512 devices in a mesh: layer: 256 (over z, y, x_lo, core), rhs: 2 (over x_hi).
Axes of the slice: x: 4 (x_hi: 2, x_lo: 2; x = x_hi * 2 + x_lo), y: 8, z: 8, core: 2. Of those that a mesh axis runs over, the one named last changes fastest.
Arguments:
- diag_block: float32 [512, 384, 384], P('layer'), may hold values from -0.234742767 to 4.6347428, as said below
- coupling: float32 [512, 384, 384], P('layer'), may hold values from -1.76123724 to 1.76123724
- right_side: float32 [512, 384, 256], P('layer', None, 'rhs'), may hold values from -6 to 6
Outputs:
- inverse_out: float32 [512, 384, 384], P('layer')
- rhs_out: float32 [512, 384, 256], P('layer', None, 'rhs')
The draws below stay inside these ranges and needn't reach their ends.
Inputs may be any that keep to these rules, and one draw needn't show every extreme that they name: `diag_block`: each diagonal block is symmetric.
All inputs are finite; a program needn't handle non-finite values.
Results may differ from the reference program's by a relative error of at most 0.00013.
Values sent between devices are 32-bit elements; how exact they have to be, the bound alone decides.
No kernel may reach another device: no remote copies, remote signals or barrier semaphores. Data moves between devices by JAX's collectives and lax.ppermute only.
A program may use at most 64 MiB of HBM per device.

```python
import math
import jax
import jax.numpy as jnp
from jax import lax

ORBITALS = 384
NS_ITERS = 3
LEVELS = 3
LAYERS = 512
RHS = 256


def draw_diag_block(key, part):
    key_noise, key_diag = jax.random.split(jax.random.fold_in(key, 11))
    spread = 0.8 / math.sqrt(ORBITALS)
    noise = jnp.clip(jax.random.normal(key_noise, (LAYERS, ORBITALS, ORBITALS), jnp.float32), -4.0, 4.0)
    symmetric = (noise + jnp.swapaxes(noise, 1, 2)) * (spread / math.sqrt(2.0))
    diagonal_vals = jax.random.uniform(key_diag, (LAYERS, ORBITALS), jnp.float32, 3.6, 4.4)
    return symmetric + diagonal_vals[:, :, None] * jnp.eye(ORBITALS, dtype=jnp.float32)[None]


def draw_coupling(key, part):
    key_noise, key_size, key_sign = jax.random.split(jax.random.fold_in(key, 23), 3)
    spread = 0.3 / math.sqrt(ORBITALS)
    noise = jnp.clip(jax.random.normal(key_noise, (LAYERS, ORBITALS, ORBITALS), jnp.float32), -4.0, 4.0)
    magnitude = jax.random.uniform(key_size, (ORBITALS,), jnp.float32, 0.9, 1.7)
    signs = jax.random.rademacher(key_sign, (LAYERS, ORBITALS), jnp.float32)
    onsite = signs * magnitude[None, :]
    return noise * spread + onsite[:, :, None] * jnp.eye(ORBITALS, dtype=jnp.float32)[None]


def levels(rng, shape, pieces, low, high):
    loudness = 1.0
    for axis_at, blocks in pieces:
        heights = jax.random.uniform(jax.random.fold_in(jax.random.fold_in(rng, 6), axis_at), (blocks,), jnp.float32, low / len(pieces), high / len(pieces))
        loudness = loudness * jnp.repeat(jnp.exp(heights), shape[axis_at] // blocks).reshape((-1,) + (1,) * (len(shape) - 1 - axis_at))
    return loudness


def centred(rng, dims, width, most, cuts=(), kind=jnp.bfloat16):
    entries = width * jax.random.normal(rng, dims, jnp.float32)
    if cuts:
        entries = entries * levels(rng, dims, cuts, -0.22, 0.18)
    return jnp.clip(entries, -most, most).astype(kind)


def setup_inputs(seed: int = 0) -> dict:
    key_of = jax.random.split(jax.random.key(seed), 4)
    return {
        "diag_block": draw_diag_block(jax.random.fold_in(key_of[3], 71), 0),
        "coupling": draw_coupling(jax.random.fold_in(key_of[3], 71), 0),
        "right_side": centred(key_of[2], (LAYERS, ORBITALS, RHS), 1.0, 6.0, ((0, 256), (2, 2)), jnp.float32),
    }


def invert(blocks):
    trace_vals = jnp.trace(blocks, axis1=1, axis2=2)
    identity = jnp.eye(ORBITALS, dtype=blocks.dtype)
    approx = identity[None] * (ORBITALS / trace_vals)[:, None, None]
    for sweep in range(NS_ITERS):
        product = jnp.einsum('bij,bjk->bik', blocks, approx, precision=lax.Precision.HIGHEST)
        approx = 2.0 * approx - jnp.einsum('bij,bjk->bik', approx, product, precision=lax.Precision.HIGHEST)
    return approx


def reference(diag_block, coupling, right_side):
    diag_now, coupling_now, rhs_now = diag_block, coupling, right_side
    inverse_out = jnp.zeros_like(diag_block)
    rhs_out = jnp.zeros_like(right_side)
    for level_num in range(LEVELS):
        stride = 2 ** level_num
        removed_idx = jnp.arange(stride - 1, LAYERS, 2 * stride)
        kept_idx = jnp.arange(2 * stride - 1, LAYERS, 2 * stride)
        approx = invert(diag_now[removed_idx])
        u_left = jnp.roll(coupling_now[kept_idx], 1, axis=0)
        u_self = coupling_now[removed_idx]
        r_self = rhs_now[removed_idx]
        stacked = jnp.concatenate([jnp.swapaxes(u_left, 1, 2), u_self, r_self], axis=2)
        solved = jnp.einsum('bij,bjk->bik', approx, stacked, precision=lax.Precision.HIGHEST)
        left_part = jnp.einsum('bij,bjk->bik', u_left, solved, precision=lax.Precision.HIGHEST)
        right_part = jnp.einsum('bji,bjk->bik', u_self, solved[:, :, ORBITALS:], precision=lax.Precision.HIGHEST)
        inverse_out = inverse_out.at[removed_idx].set(approx)
        rhs_out = rhs_out.at[removed_idx].set(r_self)
        from_right = jnp.roll(left_part, -1, axis=0)
        diag_now = diag_now.at[kept_idx].set(diag_now[kept_idx] - from_right[:, :, :ORBITALS] - right_part[:, :, :ORBITALS])
        coupling_now = coupling_now.at[kept_idx].set(-from_right[:, :, ORBITALS:2 * ORBITALS])
        rhs_now = rhs_now.at[kept_idx].set(rhs_now[kept_idx] - from_right[:, :, 2 * ORBITALS:] - right_part[:, :, ORBITALS:])
    final_idx = jnp.arange(2 ** LEVELS - 1, LAYERS, 2 ** LEVELS)
    inverse_out = inverse_out.at[final_idx].set(invert(diag_now[final_idx]))
    rhs_out = rhs_out.at[final_idx].set(rhs_now[final_idx])
    return (inverse_out, rhs_out)
```

```python
import jax
import jax.numpy as jnp
from jax import lax
from jax.experimental import pallas as pl
from jax.experimental.pallas import tpu as pltpu
from jax.sharding import PartitionSpec as P


F32 = jnp.float32
BF16 = jnp.bfloat16
N = 384
C = 128
W = 2 * N + C
MIB = 1 << 20


def eye():
    rows = lax.broadcasted_iota(jnp.int32, (N, N), 0)
    return rows == lax.broadcasted_iota(jnp.int32, (N, N), 1)


def halves(x):
    high = x.astype(BF16)
    return high, (x - high.astype(F32)).astype(BF16)


def put_left(ref, x):
    high, low = halves(x)
    ref[:, 0:N] = high
    ref[:, N : 2 * N] = high
    ref[:, 2 * N : 3 * N] = low


def put_right(ref, x, at=0):
    high, low = halves(x)
    cols = slice(at, at + x.shape[1])
    ref[0:N, cols] = high
    ref[N : 2 * N, cols] = low
    ref[2 * N : 3 * N, cols] = high


def put_right_t(ref, x):
    high, low = halves(x)
    ref[:, 0:N] = high
    ref[:, N : 2 * N] = low
    ref[:, 2 * N : 3 * N] = high


def dot(left, right):
    return jnp.dot(left, right, preferred_element_type=F32)


def dot_t(left, right):
    return lax.dot_general(
        left, right, (((1,), (1,)), ((), ())), preferred_element_type=F32
    )


def invert(block, out, left_e, left_p, right_e, right_p, s_e, s_2):
    scale = N / jnp.sum(jnp.where(eye(), block[...], 0.0))
    s_e[...] = jnp.where(eye(), 1.0, 0.0) - scale * block[...]
    put_left(left_e, s_e[...])
    put_right(right_e, s_e[...])
    s_2[...] = dot(left_e[...], right_e[...])
    put_left(left_p, s_2[...])
    put_right(right_p, s_2[...])
    put_right(right_e, dot(left_p[...], right_p[...]))
    cube = dot(left_e[...], right_p[...])
    s_e[...] = jnp.where(eye(), 1.0, 0.0) + s_e[...] + s_2[...] + cube
    put_left(left_p, s_e[...])
    out[...] = scale * (s_e[...] + dot(left_p[...], right_e[...]))


INVERT_SCRATCH = [
    pltpu.VMEM((N, 3 * N), BF16),
    pltpu.VMEM((N, 3 * N), BF16),
    pltpu.VMEM((3 * N, N), BF16),
    pltpu.VMEM((3 * N, N), BF16),
    pltpu.VMEM((N, N), F32),
    pltpu.VMEM((N, N), F32),
]


def first_kernel(diag, coup, rhs, both, inv_out, rhs_out, d_in, u_in, r_in, x_s, right, left, tmp, *rest):
    inv_scratch, sems = rest[:6], rest[6]
    core = lax.axis_index("layer") % 2
    loads = [
        pltpu.make_async_copy(diag.at[0], d_in.at[0], sems.at[0]),
        pltpu.make_async_copy(coup.at[0], u_in, sems.at[1]),
        pltpu.make_async_copy(rhs.at[0], r_in.at[0], sems.at[2]),
        pltpu.make_async_copy(diag.at[1], d_in.at[1], sems.at[3]),
        pltpu.make_async_copy(coup.at[1], both.at[core, :, N : 2 * N], sems.at[4]),
        pltpu.make_async_copy(rhs.at[1], r_in.at[1], sems.at[5]),
    ]
    for load in loads:
        load.start()
    loads[0].wait()
    invert(d_in.at[0], x_s, *inv_scratch)
    for load in loads[1:]:
        load.wait()
    stores = [
        pltpu.make_async_copy(x_s, inv_out.at[0], sems.at[0]),
        pltpu.make_async_copy(r_in.at[0], rhs_out.at[0], sems.at[1]),
    ]
    for store in stores:
        store.start()
    both[1 - core, :, 0:N] = x_s[...]
    put_left(left, x_s[...])
    put_right(right, u_in[...], 0)
    put_right(right, r_in[0], N)
    tmp[...] = dot(left[...], right[...])
    both[1 - core, :, N:W] = tmp[...]
    put_left(left, u_in[...].T)
    put_right(right, tmp[...])
    tmp[...] = dot(left[...], right[...])
    both[core, :, 0:N] = d_in[1] - tmp[:, 0:N]
    both[core, :, 2 * N : W] = r_in[1] - tmp[:, N : N + C]
    for store in stores:
        store.wait()


def second_kernel(both, recv, x_b, u_b, r_b, left, right, right_t, d_s, tmp, *inv_scratch):
    at_low = (lax.axis_index("layer") % 2) == 0
    u_s = jnp.where(at_low, both[0, :, N : 2 * N], recv[:, N : 2 * N])
    put_left(left, u_s)
    put_right_t(right_t, u_s)
    put_right(right, jnp.where(at_low, recv[...], both[0]))
    tmp[...] = dot(left[...], right[...])
    put_left(left, tmp[:, 0:N])
    d_old = jnp.where(at_low, both[0, :, 0:N], recv[:, 0:N])
    d_s[...] = d_old - dot_t(left[...], right_t[...])
    u_b[...] = -tmp[:, N : 2 * N]
    r_b[...] = jnp.where(at_low, both[0, :, 2 * N : W], recv[:, 2 * N : W]) - tmp[:, 2 * N : W]
    invert(d_s, x_b, *inv_scratch)


def third_kernel(
    both, x_b, u_b, r_b, u_l, inv_in, rhs_in, pay, full, inv_out, rhs_out, left, right, right_t, acc, tmp, w_s, sems
):
    del inv_in, rhs_in
    at_low = (lax.axis_index("layer") % 2) == 0
    stores = [
        pltpu.make_async_copy(x_b, inv_out.at[1], sems.at[0]),
        pltpu.make_async_copy(r_b, rhs_out.at[1], sems.at[1]),
    ]

    @pl.when(at_low)
    def _():
        for store in stores:
            store.start()
        put_left(left, u_l[...])
        put_right_t(right_t, u_l[...])
        put_right(right, both[1])
        tmp[...] = dot(left[...], right[...])
        put_left(left, tmp[:, 0:N])
        acc[:, 0:N] = dot_t(left[...], right_t[...])
        acc[:, N : N + C] = tmp[:, 2 * N : W]
        w_s[...] = -tmp[:, N : 2 * N]

    @pl.when(jnp.logical_not(at_low))
    def _():
        w_s[...] = u_b[...].T
        acc[:, 0:N] = -both[1, :, 0:N]
        acc[:, N : N + C] = -both[1, :, 2 * N : W]

    put_left(left, w_s[...])
    put_right_t(right_t, w_s[...])
    put_right(right, x_b[...])
    put_left(left, dot(left[...], right[:, 0:N]))
    put_right(right, u_b[...], 0)
    put_right(right, r_b[...], N)
    sign = jnp.where(at_low, 1.0, -1.0)
    pay[:, 0:N] = sign * (acc[:, 0:N] + dot_t(left[...], right_t[...]))
    tmp[:, 0 : N + C] = dot(left[...], right[:, 0 : N + C])
    pay[:, N : N + C] = sign * (acc[:, N : N + C] + tmp[:, N : N + C])

    @pl.when(at_low)
    def _():
        full[:, 0 : N + C] = pay[...]
        full[:, N + C : W] = -tmp[:, 0:N]
        for store in stores:
            store.wait()


def fourth_kernel(
    pay, other, full, inv_in, rhs_in, out, inv_out, rhs_out, left, right, right_t, d_s, x_s, r_s, w_s, *rest
):
    del inv_in, rhs_in
    inv_scratch, sems = rest[:6], rest[6]
    place = lax.axis_index("layer") % 4
    at_first = place == 1
    stores = [
        pltpu.make_async_copy(x_s, inv_out.at[1], sems.at[0]),
        pltpu.make_async_copy(r_s, rhs_out.at[1], sems.at[1]),
    ]

    @pl.when(place % 2 == 1)
    def _():
        mine = jnp.where(at_first, pay[...], other[...])
        theirs = jnp.where(at_first, other[...], full[:, 0 : N + C])
        d_s[...] = mine[:, 0:N] - theirs[:, 0:N]
        r_s[...] = mine[:, N : N + C] - theirs[:, N : N + C]
        invert(d_s, x_s, *inv_scratch)

        @pl.when(at_first)
        def _():
            for store in stores:
                store.start()
            w_s[...] = full[:, N + C : W]

        @pl.when(jnp.logical_not(at_first))
        def _():
            w_s[...] = full[:, N + C : W].T

        put_left(left, w_s[...])
        put_right_t(right_t, w_s[...])
        put_right(right, x_s[...])
        put_left(left, dot(left[...], right[...]))
        put_right(right, r_s[...])
        o_d = dot_t(left[...], right_t[...])
        out[:, 0:N] = jnp.where(at_first, full[:, 0:N] + o_d, pay[:, 0:N] - o_d)
        o_r = dot(left[...], right[:, 0:C])
        out[:, N : N + C] = jnp.where(at_first, full[:, N : N + C] + o_r, pay[:, N : N + C] - o_r)

        @pl.when(at_first)
        def _():
            for store in stores:
                store.wait()


def last_kernel(pay, other, inv_in, rhs_in, inv_out, rhs_out, d_s, x_s, r_s, *rest):
    del inv_in, rhs_in
    inv_scratch, sems = rest[:6], rest[6]

    @pl.when(lax.axis_index("layer") % 4 == 3)
    def _():
        r_s[...] = pay[:, N : N + C] - other[:, N : N + C]
        rhs_store = pltpu.make_async_copy(r_s, rhs_out.at[1], sems.at[1])
        rhs_store.start()
        d_s[...] = pay[:, 0:N] - other[:, 0:N]
        invert(d_s, x_s, *inv_scratch)
        inv_store = pltpu.make_async_copy(x_s, inv_out.at[1], sems.at[0])
        inv_store.start()
        inv_store.wait()
        rhs_store.wait()


def vmem():
    return pl.BlockSpec(memory_space=pltpu.VMEM)


def in_hbm():
    return pl.BlockSpec(memory_space=pltpu.HBM)


def like(*shape):
    return jax.ShapeDtypeStruct(shape, F32)


def call(kernel, outs, out_specs, in_specs, scratch, products, aliases=None):
    return pl.pallas_call(
        kernel,
        out_shape=outs,
        in_specs=in_specs,
        out_specs=out_specs,
        scratch_shapes=scratch,
        input_output_aliases=aliases or {},
        compiler_params=pltpu.CompilerParams(vmem_limit_bytes=28 * MIB),
        cost_estimate=pl.CostEstimate(
            flops=int(products * 6 * N * N * N), bytes_accessed=4 * MIB, transcendentals=0
        ),
    )


def reduce_chain(diag_block, coupling, right_side):
    size = lax.axis_size("layer")
    groups = range(size // 4)

    def send(block, route):
        return lax.ppermute(block, "layer", [(i % size, j % size) for i, j in route])

    wide = pltpu.VMEM((3 * N, W), BF16)
    mid = pltpu.VMEM((3 * N, N + C), BF16)
    flat = pltpu.VMEM((N, 3 * N), BF16)
    tile = pltpu.VMEM((N, N), F32)
    thin = pltpu.VMEM((N, C), F32)
    sems = pltpu.SemaphoreType.DMA((6,))
    outputs = (like(2, N, N), like(2, N, C))

    u_left = send(coupling[1], [(i, i + 1) for i in range(1, size, 2)])
    both, inv_out, rhs_out = call(
        first_kernel,
        (like(2, N, W), *outputs),
        (vmem(), in_hbm(), in_hbm()),
        [in_hbm()] * 3,
        [
            pltpu.VMEM((2, N, N), F32),
            tile,
            pltpu.VMEM((2, N, C), F32),
            tile,
            mid,
            flat,
            pltpu.VMEM((N, N + C), F32),
            *INVERT_SCRATCH,
            sems,
        ],
        6.67,
    )(*[pltpu.with_memory_space_constraint(x, pltpu.HBM) for x in (diag_block, coupling, right_side)])
    recv = send(both[0], [(i, i ^ 1) for i in range(size)])
    x_b, u_b, r_b = call(
        second_kernel,
        (like(N, N), like(N, N), like(N, C)),
        (vmem(), vmem(), vmem()),
        [vmem()] * 2,
        [flat, wide, flat, tile, pltpu.VMEM((N, W), F32), *INVERT_SCRATCH],
        7.33,
    )(both, recv)
    pay, full, inv_out, rhs_out = call(
        third_kernel,
        (like(N, N + C), like(N, W), *outputs),
        (vmem(), vmem(), in_hbm(), in_hbm()),
        [vmem()] * 5 + [in_hbm()] * 2,
        [flat, wide, flat, pltpu.VMEM((N, N + C), F32), pltpu.VMEM((N, W), F32), tile, sems],
        6.67,
        {5: 2, 6: 3},
    )(both, x_b, u_b, r_b, u_left, inv_out, rhs_out)
    across = [(4 * g + 1, 4 * g + 3) for g in groups] + [(4 * g + 2, 4 * g + 1) for g in groups]
    other = send(pay, across)
    full = send(full, [(i, i + 1) for i in range(0, size, 2)])
    out, inv_out, rhs_out = call(
        fourth_kernel,
        (like(N, N + C), *outputs),
        (vmem(), in_hbm(), in_hbm()),
        [vmem()] * 3 + [in_hbm()] * 2,
        [flat, pltpu.VMEM((3 * N, N), BF16), flat, tile, tile, thin, tile, *INVERT_SCRATCH, sems],
        6.33,
        {3: 1, 4: 2},
    )(pay, other, full, inv_out, rhs_out)
    last = send(out, [(4 * g + 5, 4 * g + 3) for g in groups])
    return call(
        last_kernel,
        outputs,
        (in_hbm(), in_hbm()),
        [vmem()] * 2 + [in_hbm()] * 2,
        [tile, tile, thin, *INVERT_SCRATCH, sems],
        4,
        {2: 0, 3: 1},
    )(out, last, inv_out, rhs_out)


def solution(mesh):
    return jax.shard_map(
        reduce_chain,
        mesh=mesh,
        in_specs=(P("layer", None, None), P("layer", None, None), P("layer", None, "rhs")),
        out_specs=(P("layer", None, None), P("layer", None, "rhs")),
        check_vma=False,
    )
```

```python
import jax
import jax.numpy as jnp
from jax import lax
from jax.experimental import pallas as pl
from jax.experimental.pallas import tpu as pltpu
from jax.sharding import PartitionSpec as P


F32 = jnp.float32
BF16 = jnp.bfloat16
N = 384
C = 128
W = 2 * N + C
MIB = 1 << 20


def eye():
    rows = lax.broadcasted_iota(jnp.int32, (N, N), 0)
    return rows == lax.broadcasted_iota(jnp.int32, (N, N), 1)


def halves(x):
    high = x.astype(BF16)
    return high, (x - high.astype(F32)).astype(BF16)


def put_left(ref, x):
    high, low = halves(x)
    ref[:, 0:N] = high
    ref[:, N : 2 * N] = high
    ref[:, 2 * N : 3 * N] = low


def put_right(ref, x, at=0):
    high, low = halves(x)
    cols = slice(at, at + x.shape[1])
    ref[0:N, cols] = high
    ref[N : 2 * N, cols] = low
    ref[2 * N : 3 * N, cols] = high


def put_right_t(ref, x):
    high, low = halves(x)
    ref[:, 0:N] = high
    ref[:, N : 2 * N] = low
    ref[:, 2 * N : 3 * N] = high


def dot(left, right):
    return jnp.dot(left, right, preferred_element_type=F32)


def dot_t(left, right):
    return lax.dot_general(
        left, right, (((1,), (1,)), ((), ())), preferred_element_type=F32
    )


def invert(block, out, left_e, left_p, right_e, right_p, s_e, s_2):
    scale = N / jnp.sum(jnp.where(eye(), block[...], 0.0))
    s_e[...] = jnp.where(eye(), 1.0, 0.0) - scale * block[...]
    put_left(left_e, s_e[...])
    put_right(right_e, s_e[...])
    s_2[...] = dot(left_e[...], right_e[...])
    put_left(left_p, s_2[...])
    put_right(right_p, s_2[...])
    put_right(right_e, dot(left_p[...], right_p[...]))
    cube = dot(left_e[...], right_p[...])
    s_e[...] = jnp.where(eye(), 1.0, 0.0) + s_e[...] + s_2[...] + cube
    put_left(left_p, s_e[...])
    out[...] = scale * (s_e[...] + dot(left_p[...], right_e[...]))


INVERT_SCRATCH = [
    pltpu.VMEM((N, 3 * N), BF16),
    pltpu.VMEM((N, 3 * N), BF16),
    pltpu.VMEM((3 * N, N), BF16),
    pltpu.VMEM((3 * N, N), BF16),
    pltpu.VMEM((N, N), F32),
    pltpu.VMEM((N, N), F32),
]


def pack(out, x):
    out[0:C, :] = x[0:C, :]
    out[C : 2 * C, 0 : 2 * C] = x[C : 2 * C, C:N]
    out[C : 2 * C, 2 * C : N] = x[2 * C : N, 2 * C : N]


def unpack(out, packed):
    out[0:C, :] = packed[0:C, :]
    out[C : 2 * C, C:N] = packed[C : 2 * C, 0 : 2 * C]
    out[2 * C : N, 2 * C : N] = packed[C : 2 * C, 2 * C : N]
    out[C : 2 * C, 0:C] = packed[0:C, C : 2 * C].T
    out[2 * C : N, 0:C] = packed[0:C, 2 * C : N].T
    out[2 * C : N, C : 2 * C] = packed[C : 2 * C, C : 2 * C].T


def pack_rhs(out, x):
    for i in range(3):
        out[2 * C : N, i * C : (i + 1) * C] = x[i * C : (i + 1) * C, :]


def unpack_rhs(packed):
    return jnp.concatenate([packed[2 * C : N, i * C : (i + 1) * C] for i in range(3)], axis=0)


def first_kernel(
    diag, coup, rhs, pay, keep, u_high, inv_out, rhs_out, d_in, u_in, r_in, x_s, right, left, *rest
):
    inv_scratch, sems = rest[:6], rest[6]
    at_low = (lax.axis_index("layer") % 2) == 0
    loads = [
        pltpu.make_async_copy(diag.at[0], d_in.at[0], sems.at[0]),
        pltpu.make_async_copy(coup.at[0], u_in, sems.at[1]),
        pltpu.make_async_copy(rhs.at[0], r_in.at[0], sems.at[2]),
        pltpu.make_async_copy(diag.at[1], d_in.at[1], sems.at[3]),
        pltpu.make_async_copy(coup.at[1], u_high, sems.at[4]),
        pltpu.make_async_copy(rhs.at[1], r_in.at[1], sems.at[5]),
    ]
    for load in loads:
        load.start()
    loads[0].wait()
    invert(d_in.at[0], x_s, *inv_scratch)
    for load in loads[1:]:
        load.wait()
    stores = [
        pltpu.make_async_copy(x_s, inv_out.at[0], sems.at[0]),
        pltpu.make_async_copy(r_in.at[0], rhs_out.at[0], sems.at[1]),
    ]
    for store in stores:
        store.start()

    def finish(of_x, of_d):
        of_x[:, 0:N] = x_s[...]
        put_left(left, x_s[...])
        put_right(right, u_in[...], 0)
        put_right(right, r_in[0], N)
        of_x[:, N:W] = dot(left[...], right[...])
        put_left(left, u_in[...].T)
        put_right(right, of_x[:, N:W])
        of_d[:, 0:N] = d_in[1] - dot(left[...], right[:, 0:N])
        of_d[:, N : 2 * N] = u_high[...]
        of_d[:, 2 * N : W] = r_in[1] - dot(left[...], right[:, N : N + C])

    @pl.when(at_low)
    def _():
        finish(keep, pay)

    @pl.when(jnp.logical_not(at_low))
    def _():
        finish(pay, keep)

    for store in stores:
        store.wait()


def second_kernel(pay, recv, x_b, u_b, r_b, left, right, right_t, d_s, tmp, *inv_scratch):
    at_low = (lax.axis_index("layer") % 2) == 0
    u_s = jnp.where(at_low, pay[:, N : 2 * N], recv[:, N : 2 * N])
    put_left(left, u_s)
    put_right_t(right_t, u_s)
    put_right(right, jnp.where(at_low, recv[...], pay[...]))
    tmp[...] = dot(left[...], right[...])
    put_left(left, tmp[:, 0:N])
    d_old = jnp.where(at_low, pay[:, 0:N], recv[:, 0:N])
    d_s[...] = d_old - dot_t(left[...], right_t[...])
    u_b[...] = -tmp[:, N : 2 * N]
    r_b[...] = jnp.where(at_low, pay[:, 2 * N : W], recv[:, 2 * N : W]) - tmp[:, 2 * N : W]
    invert(d_s, x_b, *inv_scratch)


def third_kernel(keep, x_b, u_b, r_b, packed, whole, thin, t_left, left, right, right_t, w_s):
    at_low = (lax.axis_index("layer") % 2) == 0

    @pl.when(at_low)
    def _():
        w_s[...] = keep[:, N : 2 * N]

    @pl.when(jnp.logical_not(at_low))
    def _():
        w_s[...] = u_b[...].T

    put_left(left, w_s[...])
    put_right_t(right_t, w_s[...])
    put_right(right, x_b[...])
    put_left(t_left, dot(left[...], right[...]))
    put_right(right, r_b[...])
    sign = jnp.where(at_low, 1.0, -1.0)
    whole[...] = keep[:, 0:N] + sign * dot_t(t_left[...], right_t[...])
    thin[...] = keep[:, 2 * N : W] - dot(t_left[...], right[:, 0:C])
    pack(packed, whole)
    pack_rhs(packed, thin)


def spread_kernel(t_left, u_b, r_b, whole, thin, x_b, inv_in, rhs_in, full, inv_out, rhs_out, right, sems):
    del inv_in, rhs_in

    @pl.when((lax.axis_index("layer") % 2) == 0)
    def _():
        stores = [
            pltpu.make_async_copy(x_b, inv_out.at[1], sems.at[0]),
            pltpu.make_async_copy(r_b, rhs_out.at[1], sems.at[1]),
        ]
        for store in stores:
            store.start()
        put_right(right, u_b[...])
        full[:, N : 2 * N] = dot(t_left[...], right[...])
        full[:, 0:N] = whole[...]
        full[:, 2 * N : W] = thin[...]
        for store in stores:
            store.wait()


def left_kernel(full, u_left, out, left, right, right_t):
    @pl.when((lax.axis_index("layer") % 2) == 1)
    def _():
        put_left(left, u_left[...])
        put_right_t(right_t, u_left[...])
        put_right(right, full[...])
        out[...] = dot(left[...], right[...])
        put_left(left, out[:, 0:N])
        out[:, 0:N] = dot_t(left[...], right_t[...])


def fourth_kernel(whole, packed_in, sums, u_high, packed, x_out, t_left, left, right, right_t, d_s, w_s, *inv_scratch):
    @pl.when(lax.axis_index("layer") % 4 == 1)
    def _():
        unpack(w_s, packed_in)
        put_left(left, u_high[...])
        put_right_t(right_t, u_high[...])
        put_right(right, w_s[...])
        put_left(left, dot(left[...], right[...]))
        d_s[...] = whole[...] - dot_t(left[...], right_t[...])
        invert(d_s, x_out, *inv_scratch)
        put_left(left, sums[:, N : 2 * N])
        put_right_t(right_t, sums[:, N : 2 * N])
        put_right(right, x_out[...])
        put_left(t_left, dot(left[...], right[...]))
        d_s[...] = sums[:, 0:N] + dot_t(t_left[...], right_t[...])
        pack(packed, d_s)


def fifth_kernel(
    t_left, whole, thin, packed_in, sums, u_high, x_in, inv_in, rhs_in,
    whole_out, thin_out, inv_out, rhs_out,
    left, right, right_t, d_s, x_s, w_s, r_s, *rest
):
    del inv_in, rhs_in
    inv_scratch, sems = rest[:6], rest[6]
    place = lax.axis_index("layer") % 4

    @pl.when(place == 1)
    def _():
        stores = [
            pltpu.make_async_copy(x_in, inv_out.at[1], sems.at[0]),
            pltpu.make_async_copy(r_s, rhs_out.at[1], sems.at[1]),
        ]
        stores[0].start()
        put_left(left, u_high[...])
        put_right(right, unpack_rhs(packed_in))
        r_s[...] = thin[...] - dot(left[...], right[:, 0:C])
        stores[1].start()
        put_right(right, r_s[...])
        thin_out[...] = sums[:, 2 * N : W] + dot(t_left[...], right[:, 0:C])
        for store in stores:
            store.wait()

    @pl.when(place == 3)
    def _():
        unpack(d_s, packed_in)
        d_s[...] = d_s[...] - sums[:, 0:N]
        invert(d_s, x_s, *inv_scratch)
        w_s[...] = sums[:, N : 2 * N].T
        put_left(left, w_s[...])
        put_right_t(right_t, w_s[...])
        put_right(right, x_s[...])
        put_left(left, dot(left[...], right[...]))
        whole_out[...] = whole[...] - dot_t(left[...], right_t[...])
        put_right(right, unpack_rhs(packed_in) - sums[:, 2 * N : W])
        thin_out[...] = thin[...] - dot(left[...], right[:, 0:C])


def sixth_kernel(whole, packed_in, x_out, d_s, *inv_scratch):
    @pl.when(lax.axis_index("layer") % 4 == 3)
    def _():
        unpack(d_s, packed_in)
        d_s[...] = whole[...] - d_s[...]
        invert(d_s, x_out, *inv_scratch)


def last_kernel(x_in, thin, thin_in, inv_in, rhs_in, inv_out, rhs_out, r_s, sems):
    del inv_in, rhs_in

    @pl.when(lax.axis_index("layer") % 4 == 3)
    def _():
        inv_store = pltpu.make_async_copy(x_in, inv_out.at[1], sems.at[0])
        inv_store.start()
        r_s[...] = thin[...] - thin_in[...]
        rhs_store = pltpu.make_async_copy(r_s, rhs_out.at[1], sems.at[1])
        rhs_store.start()
        inv_store.wait()
        rhs_store.wait()


def vmem():
    return pl.BlockSpec(memory_space=pltpu.VMEM)


def in_hbm():
    return pl.BlockSpec(memory_space=pltpu.HBM)


def like(*shape):
    return jax.ShapeDtypeStruct(shape, F32)


def call(kernel, outs, out_specs, in_specs, scratch, products, aliases=None):
    return pl.pallas_call(
        kernel,
        out_shape=outs,
        in_specs=in_specs,
        out_specs=out_specs,
        scratch_shapes=scratch,
        input_output_aliases=aliases or {},
        compiler_params=pltpu.CompilerParams(vmem_limit_bytes=28 * MIB),
        cost_estimate=pl.CostEstimate(
            flops=int(products * 6 * N * N * N), bytes_accessed=4 * MIB, transcendentals=0
        ),
    )


def reduce_chain(diag_block, coupling, right_side):
    size = lax.axis_size("layer")
    groups = range(size // 4)

    def send(block, route):
        return lax.ppermute(block, "layer", [(i % size, j % size) for i, j in route])

    wide = pltpu.VMEM((3 * N, W), BF16)
    mid = pltpu.VMEM((3 * N, N + C), BF16)
    tall = pltpu.VMEM((3 * N, N), BF16)
    flat = pltpu.VMEM((N, 3 * N), BF16)
    tile = pltpu.VMEM((N, N), F32)
    strip = pltpu.VMEM((N, C), F32)
    sems = pltpu.SemaphoreType.DMA((6,))
    outputs = (like(2, N, N), like(2, N, C))
    half_form = jax.ShapeDtypeStruct((N, 3 * N), BF16)
    triangle = like(2 * C, N)

    pay, keep, u_high, inv_out, rhs_out = call(
        first_kernel,
        (like(N, W), like(N, W), like(N, N), *outputs),
        (vmem(), vmem(), vmem(), in_hbm(), in_hbm()),
        [in_hbm()] * 3,
        [pltpu.VMEM((2, N, N), F32), tile, pltpu.VMEM((2, N, C), F32), tile, mid, flat, *INVERT_SCRATCH, sems],
        6.67,
    )(*[pltpu.with_memory_space_constraint(x, pltpu.HBM) for x in (diag_block, coupling, right_side)])
    recv = send(pay, [(i, i ^ 1) for i in range(size)])
    u_left = send(u_high, [(i, i + 2) for i in range(1, size, 2)])
    x_b, u_b, r_b = call(
        second_kernel,
        (like(N, N), like(N, N), like(N, C)),
        (vmem(), vmem(), vmem()),
        [vmem()] * 2,
        [flat, wide, flat, tile, pltpu.VMEM((N, W), F32), *INVERT_SCRATCH],
        7.33,
    )(pay, recv)
    packed, whole, thin, t_left = call(
        third_kernel,
        (like(N, N), like(N, N), like(N, C), half_form),
        (vmem(),) * 4,
        [vmem()] * 4,
        [flat, tall, flat, tile],
        2.33,
    )(keep, x_b, u_b, r_b)
    packed_in = send(
        packed, [(4 * g + 1, 4 * g + 3) for g in groups] + [(4 * g + 2, 4 * g + 1) for g in groups]
    )
    full, inv_out, rhs_out = call(
        spread_kernel,
        (like(N, W), *outputs),
        (vmem(), in_hbm(), in_hbm()),
        [vmem()] * 6 + [in_hbm()] * 2,
        [tall, sems],
        1,
        {6: 1, 7: 2},
    )(t_left, u_b, r_b, whole, thin, x_b, inv_out, rhs_out)
    full_in = send(full, [(i, i + 1) for i in range(0, size, 2)])
    sums = call(
        left_kernel,
        like(N, W),
        vmem(),
        [vmem()] * 2,
        [flat, wide, flat],
        3.33,
    )(full_in, u_left)
    packed, x_3, t_left = call(
        fourth_kernel,
        (triangle, like(N, N), half_form),
        (vmem(),) * 3,
        [vmem()] * 4,
        [flat, tall, flat, tile, tile, *INVERT_SCRATCH],
        8,
    )(whole, packed_in, sums, u_high)
    down = [(4 * g + 5, 4 * g + 3) for g in groups]
    last_in = send(packed, down)
    whole, thin, inv_out, rhs_out = call(
        fifth_kernel,
        (like(N, N), like(N, C), *outputs),
        (vmem(), vmem(), in_hbm(), in_hbm()),
        [vmem()] * 7 + [in_hbm()] * 2,
        [flat, tall, flat, tile, tile, tile, strip, *INVERT_SCRATCH, sems],
        6.67,
        {7: 2, 8: 3},
    )(t_left, whole, thin, packed_in, sums, u_high, x_3, inv_out, rhs_out)
    thin_in = send(thin, down)
    x_7 = call(
        sixth_kernel,
        like(N, N),
        vmem(),
        [vmem()] * 2,
        [tile, *INVERT_SCRATCH],
        4,
    )(whole, last_in)
    return call(
        last_kernel,
        outputs,
        (in_hbm(), in_hbm()),
        [vmem()] * 3 + [in_hbm()] * 2,
        [strip, sems],
        0.1,
        {3: 0, 4: 1},
    )(x_7, thin, thin_in, inv_out, rhs_out)


def solution(mesh):
    return jax.shard_map(
        reduce_chain,
        mesh=mesh,
        in_specs=(P("layer", None, None), P("layer", None, None), P("layer", None, "rhs")),
        out_specs=(P("layer", None, None), P("layer", None, "rhs")),
        check_vma=False,
    )
```

```python
import jax
import jax.numpy as jnp
from jax import lax
from jax.experimental import pallas as pl
from jax.experimental.pallas import tpu as pltpu
from jax.sharding import PartitionSpec as P


F32 = jnp.float32
BF16 = jnp.bfloat16
N = 384
C = 128
W = 2 * N + C
MIB = 1 << 20


def eye():
    rows = lax.broadcasted_iota(jnp.int32, (N, N), 0)
    return rows == lax.broadcasted_iota(jnp.int32, (N, N), 1)


def halves(x):
    high = x.astype(BF16)
    return high, (x - high.astype(F32)).astype(BF16)


def put_left(ref, x):
    high, low = halves(x)
    ref[:, 0:N] = high
    ref[:, N : 2 * N] = high
    ref[:, 2 * N : 3 * N] = low


def put_right(ref, x, at=0):
    high, low = halves(x)
    cols = slice(at, at + x.shape[1])
    ref[0:N, cols] = high
    ref[N : 2 * N, cols] = low
    ref[2 * N : 3 * N, cols] = high


def put_right_t(ref, x):
    high, low = halves(x)
    ref[:, 0:N] = high
    ref[:, N : 2 * N] = low
    ref[:, 2 * N : 3 * N] = high


def dot(left, right):
    return jnp.dot(left, right, preferred_element_type=F32)


def dot_t(left, right):
    return lax.dot_general(
        left, right, (((1,), (1,)), ((), ())), preferred_element_type=F32
    )


def invert(block, out, left_e, left_p, right_e, right_p, s_e, s_2):
    scale = N / jnp.sum(jnp.where(eye(), block[...], 0.0))
    s_e[...] = jnp.where(eye(), 1.0, 0.0) - scale * block[...]
    put_left(left_e, s_e[...])
    put_right(right_e, s_e[...])
    s_2[...] = dot(left_e[...], right_e[...])
    put_left(left_p, s_2[...])
    put_right(right_p, s_2[...])
    put_right(right_e, dot(left_p[...], right_p[...]))
    cube = dot(left_e[...], right_p[...])
    s_e[...] = jnp.where(eye(), 1.0, 0.0) + s_e[...] + s_2[...] + cube
    put_left(left_p, s_e[...])
    out[...] = scale * (s_e[...] + dot(left_p[...], right_e[...]))


INVERT_SCRATCH = [
    pltpu.VMEM((N, 3 * N), BF16),
    pltpu.VMEM((N, 3 * N), BF16),
    pltpu.VMEM((3 * N, N), BF16),
    pltpu.VMEM((3 * N, N), BF16),
    pltpu.VMEM((N, N), F32),
    pltpu.VMEM((N, N), F32),
]


def pack(out, x):
    out[0:C, :] = x[0:C, :]
    out[C : 2 * C, 0 : 2 * C] = x[C : 2 * C, C:N]
    out[C : 2 * C, 2 * C : N] = x[2 * C : N, 2 * C : N]


def unpack(out, packed):
    out[0:C, :] = packed[0:C, :]
    out[C : 2 * C, C:N] = packed[C : 2 * C, 0 : 2 * C]
    out[2 * C : N, 2 * C : N] = packed[C : 2 * C, 2 * C : N]
    out[C : 2 * C, 0:C] = packed[0:C, C : 2 * C].T
    out[2 * C : N, 0:C] = packed[0:C, 2 * C : N].T
    out[2 * C : N, C : 2 * C] = packed[C : 2 * C, C : 2 * C].T


def pack_rhs(out, x):
    for i in range(3):
        out[2 * C : N, i * C : (i + 1) * C] = x[i * C : (i + 1) * C, :]


def unpack_rhs(packed):
    return jnp.concatenate([packed[2 * C : N, i * C : (i + 1) * C] for i in range(3)], axis=0)


def first_kernel(
    diag, coup, rhs, pay, keep, u_high, inv_out, rhs_out, d_in, u_in, r_in, x_s, right, left, *rest
):
    inv_scratch, sems = rest[:6], rest[6]
    at_low = (lax.axis_index("layer") % 2) == 0
    loads = [
        pltpu.make_async_copy(diag.at[0], d_in.at[0], sems.at[0]),
        pltpu.make_async_copy(coup.at[0], u_in, sems.at[1]),
        pltpu.make_async_copy(rhs.at[0], r_in.at[0], sems.at[2]),
        pltpu.make_async_copy(diag.at[1], d_in.at[1], sems.at[3]),
        pltpu.make_async_copy(coup.at[1], u_high, sems.at[4]),
        pltpu.make_async_copy(rhs.at[1], r_in.at[1], sems.at[5]),
    ]
    for load in loads:
        load.start()
    loads[0].wait()
    invert(d_in.at[0], x_s, *inv_scratch)
    for load in loads[1:]:
        load.wait()
    stores = [
        pltpu.make_async_copy(x_s, inv_out.at[0], sems.at[0]),
        pltpu.make_async_copy(r_in.at[0], rhs_out.at[0], sems.at[1]),
    ]
    for store in stores:
        store.start()

    def finish(of_x, of_d):
        of_x[:, 0:N] = x_s[...]
        put_left(left, x_s[...])
        put_right(right, u_in[...], 0)
        put_right(right, r_in[0], N)
        of_x[:, N:W] = dot(left[...], right[...])
        put_left(left, u_in[...].T)
        put_right(right, of_x[:, N:W])
        of_d[:, 0:N] = d_in[1] - dot(left[...], right[:, 0:N])
        of_d[:, N : 2 * N] = u_high[...]
        of_d[:, 2 * N : W] = r_in[1] - dot(left[...], right[:, N : N + C])

    @pl.when(at_low)
    def _():
        finish(keep, pay)

    @pl.when(jnp.logical_not(at_low))
    def _():
        finish(pay, keep)

    for store in stores:
        store.wait()


def second_kernel(pay, recv, x_b, u_b, r_b, left, right, right_t, d_s, tmp, *inv_scratch):
    at_low = (lax.axis_index("layer") % 2) == 0
    u_s = jnp.where(at_low, pay[:, N : 2 * N], recv[:, N : 2 * N])
    put_left(left, u_s)
    put_right_t(right_t, u_s)
    put_right(right, jnp.where(at_low, recv[...], pay[...]))
    tmp[...] = dot(left[...], right[...])
    put_left(left, tmp[:, 0:N])
    d_old = jnp.where(at_low, pay[:, 0:N], recv[:, 0:N])
    d_s[...] = d_old - dot_t(left[...], right_t[...])
    u_b[...] = -tmp[:, N : 2 * N]
    r_b[...] = jnp.where(at_low, pay[:, 2 * N : W], recv[:, 2 * N : W]) - tmp[:, 2 * N : W]
    invert(d_s, x_b, *inv_scratch)


def third_kernel(keep, x_b, r_b, packed, whole, thin, t_left, left, right, right_t):
    @pl.when((lax.axis_index("layer") % 2) == 0)
    def _():
        put_left(left, keep[:, N : 2 * N])
        put_right_t(right_t, keep[:, N : 2 * N])
        put_right(right, x_b[...])
        put_left(t_left, dot(left[...], right[...]))
        put_right(right, r_b[...])
        thin[...] = keep[:, 2 * N : W] - dot(t_left[...], right[:, 0:C])
        pack_rhs(packed, thin)
        whole[...] = keep[:, 0:N] + dot_t(t_left[...], right_t[...])
        pack(packed, whole)


def spread_kernel(
    t_left, u_b, r_b, keep, s_in, thin_in, x_b, inv_in, rhs_in,
    full, packed, whole, thin, inv_out, rhs_out, left, right, right_t, w_s, sems
):
    del inv_in, rhs_in
    at_low = (lax.axis_index("layer") % 2) == 0

    @pl.when(at_low)
    def _():
        stores = [
            pltpu.make_async_copy(x_b, inv_out.at[1], sems.at[0]),
            pltpu.make_async_copy(r_b, rhs_out.at[1], sems.at[1]),
        ]
        for store in stores:
            store.start()
        put_right(right, u_b[...])
        full[:, N : 2 * N] = dot(t_left[...], right[...])
        full[:, 0:N] = s_in[...]
        full[:, 2 * N : W] = thin_in[...]
        for store in stores:
            store.wait()

    @pl.when(jnp.logical_not(at_low))
    def _():
        w_s[...] = u_b[...].T
        put_left(left, w_s[...])
        put_right_t(right_t, w_s[...])
        put_right(right, x_b[...])
        put_left(left, dot(left[...], right[...]))
        put_right(right, r_b[...])
        whole[...] = keep[:, 0:N] - dot_t(left[...], right_t[...])
        thin[...] = keep[:, 2 * N : W] - dot(left[...], right[:, 0:C])
        pack(packed, whole)
        pack_rhs(packed, thin)


def left_kernel(full, u_left, out, left, right, right_t):
    @pl.when((lax.axis_index("layer") % 2) == 1)
    def _():
        put_left(left, u_left[...])
        put_right_t(right_t, u_left[...])
        put_right(right, full[...])
        out[...] = dot(left[...], right[...])
        put_left(left, out[:, 0:N])
        out[:, 0:N] = dot_t(left[...], right_t[...])


def fourth_kernel(
    whole, thin, packed_in, sums, u_high, packed, thin_out, x_out, r_out, left, right, right_t, d_s, *inv_scratch
):
    @pl.when(lax.axis_index("layer") % 4 == 1)
    def _():
        put_left(left, u_high[...])
        put_right_t(right_t, u_high[...])
        put_right(right, unpack_rhs(packed_in))
        r_out[...] = thin[...] - dot(left[...], right[:, 0:C])
        unpack(d_s, packed_in)
        put_right(right, d_s[...])
        put_left(left, dot(left[...], right[...]))
        d_s[...] = whole[...] - dot_t(left[...], right_t[...])
        invert(d_s, x_out, *inv_scratch)
        put_left(left, sums[:, N : 2 * N])
        put_right_t(right_t, sums[:, N : 2 * N])
        put_right(right, x_out[...])
        put_left(left, dot(left[...], right[...]))
        put_right(right, r_out[...])
        d_s[...] = sums[:, 0:N] + dot_t(left[...], right_t[...])
        thin_out[...] = sums[:, 2 * N : W] + dot(left[...], right[:, 0:C])
        pack(packed, d_s)


def fifth_kernel(
    whole, thin, packed_in, sums, x_in, r_in, inv_in, rhs_in,
    whole_out, thin_out, inv_out, rhs_out,
    left, right, right_t, d_s, x_s, w_s, *rest
):
    del inv_in, rhs_in
    inv_scratch, sems = rest[:6], rest[6]
    place = lax.axis_index("layer") % 4

    @pl.when(place == 1)
    def _():
        stores = [
            pltpu.make_async_copy(x_in, inv_out.at[1], sems.at[0]),
            pltpu.make_async_copy(r_in, rhs_out.at[1], sems.at[1]),
        ]
        for store in stores:
            store.start()
        for store in stores:
            store.wait()

    @pl.when(place == 3)
    def _():
        unpack(d_s, packed_in)
        d_s[...] = d_s[...] - sums[:, 0:N]
        invert(d_s, x_s, *inv_scratch)
        w_s[...] = sums[:, N : 2 * N].T
        put_left(left, w_s[...])
        put_right_t(right_t, w_s[...])
        put_right(right, x_s[...])
        put_left(left, dot(left[...], right[...]))
        whole_out[...] = whole[...] - dot_t(left[...], right_t[...])
        put_right(right, unpack_rhs(packed_in) - sums[:, 2 * N : W])
        thin_out[...] = thin[...] - dot(left[...], right[:, 0:C])


def sixth_kernel(whole, packed_in, x_out, d_s, *inv_scratch):
    @pl.when(lax.axis_index("layer") % 4 == 3)
    def _():
        unpack(d_s, packed_in)
        d_s[...] = whole[...] - d_s[...]
        invert(d_s, x_out, *inv_scratch)


def last_kernel(x_in, thin, thin_in, inv_in, rhs_in, inv_out, rhs_out, r_s, sems):
    del inv_in, rhs_in

    @pl.when(lax.axis_index("layer") % 4 == 3)
    def _():
        inv_store = pltpu.make_async_copy(x_in, inv_out.at[1], sems.at[0])
        inv_store.start()
        r_s[...] = thin[...] - thin_in[...]
        rhs_store = pltpu.make_async_copy(r_s, rhs_out.at[1], sems.at[1])
        rhs_store.start()
        inv_store.wait()
        rhs_store.wait()


def vmem():
    return pl.BlockSpec(memory_space=pltpu.VMEM)


def in_hbm():
    return pl.BlockSpec(memory_space=pltpu.HBM)


def like(*shape):
    return jax.ShapeDtypeStruct(shape, F32)


def call(kernel, outs, out_specs, in_specs, scratch, products, aliases=None):
    return pl.pallas_call(
        kernel,
        out_shape=outs,
        in_specs=in_specs,
        out_specs=out_specs,
        scratch_shapes=scratch,
        input_output_aliases=aliases or {},
        compiler_params=pltpu.CompilerParams(vmem_limit_bytes=28 * MIB),
        cost_estimate=pl.CostEstimate(
            flops=int(products * 6 * N * N * N), bytes_accessed=4 * MIB, transcendentals=0
        ),
    )


def reduce_chain(diag_block, coupling, right_side):
    size = lax.axis_size("layer")
    groups = range(size // 4)

    def send(block, route):
        return lax.ppermute(block, "layer", [(i % size, j % size) for i, j in route])

    wide = pltpu.VMEM((3 * N, W), BF16)
    mid = pltpu.VMEM((3 * N, N + C), BF16)
    tall = pltpu.VMEM((3 * N, N), BF16)
    flat = pltpu.VMEM((N, 3 * N), BF16)
    tile = pltpu.VMEM((N, N), F32)
    strip = pltpu.VMEM((N, C), F32)
    sems = pltpu.SemaphoreType.DMA((6,))
    outputs = (like(2, N, N), like(2, N, C))
    half_form = jax.ShapeDtypeStruct((N, 3 * N), BF16)
    triangle = like(2 * C, N)

    pay, keep, u_high, inv_out, rhs_out = call(
        first_kernel,
        (like(N, W), like(N, W), like(N, N), *outputs),
        (vmem(), vmem(), vmem(), in_hbm(), in_hbm()),
        [in_hbm()] * 3,
        [pltpu.VMEM((2, N, N), F32), tile, pltpu.VMEM((2, N, C), F32), tile, mid, flat, *INVERT_SCRATCH, sems],
        6.67,
    )(*[pltpu.with_memory_space_constraint(x, pltpu.HBM) for x in (diag_block, coupling, right_side)])
    recv = send(pay, [(i, i ^ 1) for i in range(size)])
    u_left = send(u_high, [(i, i + 2) for i in range(1, size, 2)])
    x_b, u_b, r_b = call(
        second_kernel,
        (like(N, N), like(N, N), like(N, C)),
        (vmem(), vmem(), vmem()),
        [vmem()] * 2,
        [flat, wide, flat, tile, pltpu.VMEM((N, W), F32), *INVERT_SCRATCH],
        7.33,
    )(pay, recv)
    packed, whole, thin, t_left = call(
        third_kernel,
        (like(N, N), like(N, N), like(N, C), half_form),
        (vmem(),) * 4,
        [vmem()] * 3,
        [flat, tall, flat],
        2.33,
    )(keep, x_b, r_b)
    urgent_in = send(packed, [(4 * g + 2, 4 * g + 1) for g in groups])
    full, packed, whole, thin, inv_out, rhs_out = call(
        spread_kernel,
        (like(N, W), like(N, N), like(N, N), like(N, C), *outputs),
        (vmem(), vmem(), vmem(), vmem(), in_hbm(), in_hbm()),
        [vmem()] * 7 + [in_hbm()] * 2,
        [flat, tall, flat, tile, sems],
        2,
        {7: 4, 8: 5},
    )(t_left, u_b, r_b, keep, whole, thin, x_b, inv_out, rhs_out)
    full_in = send(full, [(i, i + 1) for i in range(0, size, 2)])
    packed_in = send(packed, [(4 * g + 1, 4 * g + 3) for g in groups])
    sums = call(
        left_kernel,
        like(N, W),
        vmem(),
        [vmem()] * 2,
        [flat, wide, flat],
        3.33,
    )(full_in, u_left)
    packed, down_thin, x_3, r_3 = call(
        fourth_kernel,
        (triangle, like(N, C), like(N, N), like(N, C)),
        (vmem(),) * 4,
        [vmem()] * 5,
        [flat, tall, flat, tile, *INVERT_SCRATCH],
        8.67,
    )(whole, thin, urgent_in, sums, u_high)
    down = [(4 * g + 5, 4 * g + 3) for g in groups]
    last_in = send(packed, down)
    thin_in = send(down_thin, down)
    whole, thin, inv_out, rhs_out = call(
        fifth_kernel,
        (like(N, N), like(N, C), *outputs),
        (vmem(), vmem(), in_hbm(), in_hbm()),
        [vmem()] * 6 + [in_hbm()] * 2,
        [flat, tall, flat, tile, tile, tile, *INVERT_SCRATCH, sems],
        6.67,
        {6: 2, 7: 3},
    )(whole, thin, packed_in, sums, x_3, r_3, inv_out, rhs_out)
    x_7 = call(
        sixth_kernel,
        like(N, N),
        vmem(),
        [vmem()] * 2,
        [tile, *INVERT_SCRATCH],
        4,
    )(whole, last_in)
    return call(
        last_kernel,
        outputs,
        (in_hbm(), in_hbm()),
        [vmem()] * 3 + [in_hbm()] * 2,
        [strip, sems],
        0.1,
        {3: 0, 4: 1},
    )(x_7, thin, thin_in, inv_out, rhs_out)


def solution(mesh):
    return jax.shard_map(
        reduce_chain,
        mesh=mesh,
        in_specs=(P("layer", None, None), P("layer", None, None), P("layer", None, "rhs")),
        out_specs=(P("layer", None, None), P("layer", None, "rhs")),
        check_vma=False,
    )
```

```python
import jax
import jax.numpy as jnp
from jax import lax
from jax.experimental import pallas as pl
from jax.experimental.pallas import tpu as pltpu
from jax.sharding import PartitionSpec as P


F32 = jnp.float32
BF16 = jnp.bfloat16
N = 384
C = 128
W = 2 * N + C
MIB = 1 << 20


def eye():
    rows = lax.broadcasted_iota(jnp.int32, (N, N), 0)
    return rows == lax.broadcasted_iota(jnp.int32, (N, N), 1)


def halves(x):
    high = x.astype(BF16)
    return high, (x - high.astype(F32)).astype(BF16)


def put_left(ref, x):
    high, low = halves(x)
    ref[:, 0:N] = high
    ref[:, N : 2 * N] = high
    ref[:, 2 * N : 3 * N] = low


def put_right(ref, x, at=0):
    high, low = halves(x)
    cols = slice(at, at + x.shape[1])
    ref[0:N, cols] = high
    ref[N : 2 * N, cols] = low
    ref[2 * N : 3 * N, cols] = high


def put_both(ref, x):
    high, low = halves(x)
    ref[:, 0:N] = high
    ref[:, N : 2 * N] = high
    ref[:, 2 * N : 3 * N] = low
    ref[:, 3 * N : 4 * N] = high


def dot(left, right):
    return jnp.dot(left, right, preferred_element_type=F32)


def dot_t(left, right):
    return lax.dot_general(
        left, right, (((1,), (1,)), ((), ())), preferred_element_type=F32
    )


def as_left(ref):
    return ref[:, 0 : 3 * N]


def as_right_t(ref):
    return ref[:, N : 4 * N]


def invert(block, out, left_e, left_p, right_e, right_p, s_e, s_2, beside=None):
    scale = N / jnp.sum(jnp.where(eye(), block[...], 0.0))
    s_e[...] = jnp.where(eye(), 1.0, 0.0) - scale * block[...]
    put_left(left_e, s_e[...])
    put_right(right_e, s_e[...])
    s_2[...] = dot(left_e[...], right_e[...])
    if beside is not None:
        beside()
    put_left(left_p, s_2[...])
    put_right(right_p, s_2[...])
    put_right(right_e, dot(left_p[...], right_p[...]))
    cube = dot(left_e[...], right_p[...])
    s_e[...] = jnp.where(eye(), 1.0, 0.0) + s_e[...] + s_2[...] + cube
    put_left(left_p, s_e[...])
    out[...] = scale * (s_e[...] + dot(left_p[...], right_e[...]))


INVERT_SCRATCH = [
    pltpu.VMEM((N, 3 * N), BF16),
    pltpu.VMEM((N, 3 * N), BF16),
    pltpu.VMEM((3 * N, N), BF16),
    pltpu.VMEM((3 * N, N), BF16),
    pltpu.VMEM((N, N), F32),
    pltpu.VMEM((N, N), F32),
]


def pack(out, x):
    out[0:C, :] = x[0:C, :]
    out[C : 2 * C, 0 : 2 * C] = x[C : 2 * C, C:N]
    out[C : 2 * C, 2 * C : N] = x[2 * C : N, 2 * C : N]


def unpack(out, packed):
    out[0:C, :] = packed[0:C, :]
    out[C : 2 * C, C:N] = packed[C : 2 * C, 0 : 2 * C]
    out[2 * C : N, 2 * C : N] = packed[C : 2 * C, 2 * C : N]
    out[C : 2 * C, 0:C] = packed[0:C, C : 2 * C].T
    out[2 * C : N, 0:C] = packed[0:C, 2 * C : N].T
    out[2 * C : N, C : 2 * C] = packed[C : 2 * C, C : 2 * C].T


def pack_rhs(out, x):
    for i in range(3):
        out[2 * C : N, i * C : (i + 1) * C] = x[i * C : (i + 1) * C, :]


def unpack_rhs(packed):
    return jnp.concatenate([packed[2 * C : N, i * C : (i + 1) * C] for i in range(3)], axis=0)


def first_kernel(
    diag, coup, rhs, pay, keep, u_high, inv_out, rhs_out, d_in, u_in, r_in, right, left, left_u, *rest
):
    inv_scratch, sems = rest[:6], rest[6]
    at_low = (lax.axis_index("layer") % 2) == 0
    loads = [
        pltpu.make_async_copy(diag.at[0], d_in.at[0], sems.at[0]),
        pltpu.make_async_copy(coup.at[0], u_in, sems.at[1]),
        pltpu.make_async_copy(rhs.at[0], r_in.at[0], sems.at[2]),
        pltpu.make_async_copy(diag.at[1], d_in.at[1], sems.at[3]),
        pltpu.make_async_copy(coup.at[1], u_high, sems.at[4]),
        pltpu.make_async_copy(rhs.at[1], r_in.at[1], sems.at[5]),
    ]
    loads[0].start()
    loads[1].start()
    loads[0].wait()
    for load in loads[2:]:
        load.start()
    loads[1].wait()

    def transpose_u():
        put_left(left_u, u_in[...].T)
        put_right(right, u_in[...], 0)

    def finish(of_x, of_d):
        invert(d_in.at[0], of_x.at[:, 0:N], *inv_scratch, beside=transpose_u)
        for load in loads[2:]:
            load.wait()
        stores = [
            pltpu.make_async_copy(of_x.at[:, 0:N], inv_out.at[0], sems.at[0]),
            pltpu.make_async_copy(r_in.at[0], rhs_out.at[0], sems.at[1]),
        ]
        for store in stores:
            store.start()
        put_left(left, of_x[:, 0:N])
        put_right(right, r_in[0], N)
        of_x[:, N:W] = dot(left[...], right[...])
        put_right(right, of_x[:, N:W])
        of_d[:, 0:N] = d_in[1] - dot(left_u[...], right[:, 0:N])
        of_d[:, 2 * N : W] = r_in[1] - dot(left_u[...], right[:, N : N + C])
        for store in stores:
            store.wait()

    @pl.when(at_low)
    def _():
        finish(keep, pay)
        pay[:, N : 2 * N] = u_high[...]

    @pl.when(jnp.logical_not(at_low))
    def _():
        finish(pay, keep)


def by_role(step, pay, recv):
    at_low = (lax.axis_index("layer") % 2) == 0

    @pl.when(at_low)
    def _():
        step(pay, recv)

    @pl.when(jnp.logical_not(at_low))
    def _():
        step(recv, pay)


def second_kernel(pay, recv, x_b, both, left, right, d_s, *inv_scratch):
    def step(of_d, of_x):
        put_both(both, of_d[:, N : 2 * N])
        put_right(right, of_x[:, 0:N])
        put_left(left, dot(as_left(both), right[...]))
        d_s[...] = of_d[:, 0:N] - dot_t(left[...], as_right_t(both))

    by_role(step, pay, recv)
    invert(d_s, x_b, *inv_scratch)


def third_kernel(keep, x_b, packed, whole, t_left, both, right):
    @pl.when((lax.axis_index("layer") % 2) == 0)
    def _():
        put_both(both, keep[:, N : 2 * N])
        put_right(right, x_b[...])
        put_left(t_left, dot(as_left(both), right[...]))
        whole[...] = keep[:, 0:N] + dot_t(t_left[...], as_right_t(both))
        pack(packed, whole)


def spread_kernel(
    t_left, pay, recv, keep, s_in, x_b, inv_in, rhs_in,
    full, packed, whole, thin, inv_out, rhs_out, both, left, right, u_b, r_b, sems
):
    del inv_in, rhs_in
    at_low = (lax.axis_index("layer") % 2) == 0
    stores = [
        pltpu.make_async_copy(x_b, inv_out.at[1], sems.at[0]),
        pltpu.make_async_copy(r_b, rhs_out.at[1], sems.at[1]),
    ]

    def step(of_d, of_x):
        put_left(left, of_d[:, N : 2 * N])
        put_right(right, of_x[:, N:W])
        u_b[...] = -dot(left[...], right[:, 0:N])
        r_b[...] = of_d[:, 2 * N : W] - dot(left[...], right[:, N : N + C])

    by_role(step, pay, recv)

    @pl.when(at_low)
    def _():
        for store in stores:
            store.start()
        put_right(right, u_b[...], 0)
        put_right(right, r_b[...], N)
        full[:, N : 2 * N] = dot(t_left[...], right[:, 0:N])
        thin[...] = keep[:, 2 * N : W] - dot(t_left[...], right[:, N : N + C])
        full[:, 0:N] = s_in[...]
        full[:, 2 * N : W] = thin[...]
        for store in stores:
            store.wait()

    @pl.when(jnp.logical_not(at_low))
    def _():
        put_both(both, u_b[...].T)
        put_right(right, x_b[...], 0)
        put_left(left, dot(as_left(both), right[:, 0:N]))
        put_right(right, r_b[...], N)
        whole[...] = keep[:, 0:N] - dot_t(left[...], as_right_t(both))
        thin[...] = keep[:, 2 * N : W] - dot(left[...], right[:, N : N + C])
        pack(packed, whole)
        pack_rhs(packed, thin)


def fourth_kernel(whole, packed_in, full, u_high, packed, x_out, t_left, both, left, right, d_s, *inv_scratch):
    @pl.when(lax.axis_index("layer") % 4 == 1)
    def _():
        put_both(both, u_high[...])
        unpack(d_s, packed_in)
        put_right(right, d_s[...])
        put_left(left, dot(as_left(both), right[...]))
        d_s[...] = whole[...] - dot_t(left[...], as_right_t(both))
        invert(d_s, x_out, *inv_scratch, beside=lambda: put_both(both, full[:, N : 2 * N]))
        put_right(right, x_out[...])
        put_left(t_left, dot(as_left(both), right[...]))
        d_s[...] = full[:, 0:N] + dot_t(t_left[...], as_right_t(both))
        pack(packed, d_s)


def rest_kernel(t_left, thin, thin_in, full, u_high, thin_out, r_out, left, right):
    @pl.when(lax.axis_index("layer") % 4 == 1)
    def _():
        put_left(left, u_high[...])
        put_right(right, thin_in[...])
        r_out[...] = thin[...] - dot(left[...], right[...])
        put_right(right, r_out[...])
        thin_out[...] = full[:, 2 * N : W] + dot(t_left[...], right[...])


def left_kernel(full, u_left, sums, both, left, right):
    @pl.when(lax.axis_index("layer") % 4 == 3)
    def _():
        put_both(both, u_left[...])
        put_right(right, full[...])
        sums[...] = dot(as_left(both), right[...])
        put_left(left, sums[:, 0:N])
        sums[:, 0:N] = dot_t(left[...], as_right_t(both))


def fifth_kernel(
    whole, thin, packed_in, sums, u_high, x_in, r_in, inv_in, rhs_in,
    whole_out, thin_out, u_both, inv_out, rhs_out,
    both, left, right, d_s, x_s, *rest
):
    del inv_in, rhs_in
    inv_scratch, sems = rest[:6], rest[6]
    place = lax.axis_index("layer") % 4

    @pl.when(place == 1)
    def _():
        stores = [
            pltpu.make_async_copy(x_in, inv_out.at[1], sems.at[0]),
            pltpu.make_async_copy(r_in, rhs_out.at[1], sems.at[1]),
        ]
        for store in stores:
            store.start()
        for store in stores:
            store.wait()

    @pl.when(place == 3)
    def _():
        unpack(d_s, packed_in)
        d_s[...] = d_s[...] - sums[:, 0:N]
        invert(d_s, x_s, *inv_scratch, beside=lambda: put_both(both, sums[:, N : 2 * N].T))
        put_right(right, x_s[...])
        put_left(left, dot(as_left(both), right[...]))
        whole_out[...] = whole[...] - dot_t(left[...], as_right_t(both))
        put_right(right, unpack_rhs(packed_in) - sums[:, 2 * N : W])
        thin_out[...] = thin[...] - dot(left[...], right[:, 0:C])
        put_both(u_both, u_high[...])


def sixth_kernel(whole, packed_in, u_both, x_out, left, right, d_s, *inv_scratch):
    @pl.when(lax.axis_index("layer") % 4 == 3)
    def _():
        unpack(d_s, packed_in)
        put_right(right, d_s[...])
        put_left(left, dot(as_left(u_both), right[...]))
        d_s[...] = whole[...] - dot_t(left[...], as_right_t(u_both))
        invert(d_s, x_out, *inv_scratch)


def last_kernel(x_in, thin, thin_in, u_both, inv_in, rhs_in, inv_out, rhs_out, right, r_s, sems):
    del inv_in, rhs_in

    @pl.when(lax.axis_index("layer") % 4 == 3)
    def _():
        inv_store = pltpu.make_async_copy(x_in, inv_out.at[1], sems.at[0])
        inv_store.start()
        put_right(right, thin_in[...])
        r_s[...] = thin[...] - dot(as_left(u_both), right[...])
        rhs_store = pltpu.make_async_copy(r_s, rhs_out.at[1], sems.at[1])
        rhs_store.start()
        inv_store.wait()
        rhs_store.wait()


def vmem():
    return pl.BlockSpec(memory_space=pltpu.VMEM)


def in_hbm():
    return pl.BlockSpec(memory_space=pltpu.HBM)


def like(*shape):
    return jax.ShapeDtypeStruct(shape, F32)


def call(kernel, outs, out_specs, in_specs, scratch, products, aliases=None):
    return pl.pallas_call(
        kernel,
        out_shape=outs,
        in_specs=in_specs,
        out_specs=out_specs,
        scratch_shapes=scratch,
        input_output_aliases=aliases or {},
        compiler_params=pltpu.CompilerParams(vmem_limit_bytes=28 * MIB),
        cost_estimate=pl.CostEstimate(
            flops=int(products * 6 * N * N * N), bytes_accessed=4 * MIB, transcendentals=0
        ),
    )


def reduce_chain(diag_block, coupling, right_side):
    size = lax.axis_size("layer")
    groups = range(size // 4)

    def send(block, route):
        return lax.ppermute(block, "layer", [(i % size, j % size) for i, j in route])

    def send_crossed(block, route):
        pairs = [(2 * (i % size) + c, 2 * (j % size) + 1 - c) for i, j in route for c in (0, 1)]
        return lax.ppermute(block, ("layer", "rhs"), pairs)

    wide = pltpu.VMEM((3 * N, W), BF16)
    mid = pltpu.VMEM((3 * N, N + C), BF16)
    tall = pltpu.VMEM((3 * N, N), BF16)
    flat = pltpu.VMEM((N, 3 * N), BF16)
    double = pltpu.VMEM((N, 4 * N), BF16)
    tile = pltpu.VMEM((N, N), F32)
    strip = pltpu.VMEM((N, C), F32)
    sems = pltpu.SemaphoreType.DMA((6,))
    outputs = (like(2, N, N), like(2, N, C))
    half_form = jax.ShapeDtypeStruct((N, 3 * N), BF16)
    triangle = like(2 * C, N)

    pay, keep, u_high, inv_out, rhs_out = call(
        first_kernel,
        (like(N, W), like(N, W), like(N, N), *outputs),
        (vmem(), vmem(), vmem(), in_hbm(), in_hbm()),
        [in_hbm()] * 3,
        [pltpu.VMEM((2, N, N), F32), tile, pltpu.VMEM((2, N, C), F32), mid, flat, flat, *INVERT_SCRATCH, sems],
        6.67,
    )(*[pltpu.with_memory_space_constraint(x, pltpu.HBM) for x in (diag_block, coupling, right_side)])
    recv = send(pay, [(i, i ^ 1) for i in range(size)])
    u_left = send(u_high, [(4 * g + 1, 4 * g + 3) for g in groups])
    x_b = call(
        second_kernel,
        like(N, N),
        vmem(),
        [vmem()] * 2,
        [double, flat, tall, tile, *INVERT_SCRATCH],
        6,
    )(pay, recv)
    packed, whole, t_left = call(
        third_kernel,
        (triangle, like(N, N), half_form),
        (vmem(),) * 3,
        [vmem()] * 2,
        [double, tall],
        2,
    )(keep, x_b)
    urgent_in = send_crossed(packed, [(4 * g + 2, 4 * g + 1) for g in groups])
    full, packed, whole, thin, inv_out, rhs_out = call(
        spread_kernel,
        (like(N, W), like(N, N), like(N, N), like(N, C), *outputs),
        (vmem(), vmem(), vmem(), vmem(), in_hbm(), in_hbm()),
        [vmem()] * 6 + [in_hbm()] * 2,
        [double, flat, mid, tile, strip, sems],
        3.33,
        {6: 4, 7: 5},
    )(t_left, pay, recv, keep, whole, x_b, inv_out, rhs_out)
    full_in = send(full, [(4 * g, 4 * g + 1) for g in groups])
    thin_in = send(thin, [(4 * g + 2, 4 * g + 1) for g in groups])
    packed_in = send(packed, [(4 * g + 1, 4 * g + 3) for g in groups])
    packed, x_3, t_left = call(
        fourth_kernel,
        (triangle, like(N, N), half_form),
        (vmem(),) * 3,
        [vmem()] * 4,
        [double, flat, tall, tile, *INVERT_SCRATCH],
        8,
    )(whole, urgent_in, full_in, u_high)
    down = [(4 * g + 5, 4 * g + 3) for g in groups]
    last_in = send_crossed(packed, down)
    down_thin, r_3 = call(
        rest_kernel,
        (like(N, C), like(N, C)),
        (vmem(),) * 2,
        [vmem()] * 5,
        [flat, pltpu.VMEM((3 * N, C), BF16)],
        0.67,
    )(t_left, thin, thin_in, full_in, u_high)
    thin_in = send(down_thin, down)
    sums = call(
        left_kernel,
        like(N, W),
        vmem(),
        [vmem()] * 2,
        [double, flat, wide],
        3.33,
    )(send(full, [(4 * g + 2, 4 * g + 3) for g in groups]), u_left)
    whole, thin, u_both, inv_out, rhs_out = call(
        fifth_kernel,
        (like(N, N), like(N, C), jax.ShapeDtypeStruct((N, 4 * N), BF16), *outputs),
        (vmem(), vmem(), vmem(), in_hbm(), in_hbm()),
        [vmem()] * 7 + [in_hbm()] * 2,
        [double, flat, tall, tile, tile, *INVERT_SCRATCH, sems],
        6.33,
        {7: 3, 8: 4},
    )(whole, thin, packed_in, sums, u_high, x_3, r_3, inv_out, rhs_out)
    x_7 = call(
        sixth_kernel,
        like(N, N),
        vmem(),
        [vmem()] * 3,
        [flat, tall, tile, *INVERT_SCRATCH],
        6,
    )(whole, last_in, u_both)
    return call(
        last_kernel,
        outputs,
        (in_hbm(), in_hbm()),
        [vmem()] * 4 + [in_hbm()] * 2,
        [pltpu.VMEM((3 * N, C), BF16), strip, sems],
        0.33,
        {4: 0, 5: 1},
    )(x_7, thin, thin_in, u_both, inv_out, rhs_out)


def solution(mesh):
    return jax.shard_map(
        reduce_chain,
        mesh=mesh,
        in_specs=(P("layer", None, None), P("layer", None, None), P("layer", None, "rhs")),
        out_specs=(P("layer", None, None), P("layer", None, "rhs")),
        check_vma=False,
    )
```

```python
import jax
import jax.numpy as jnp
from jax import lax
from jax.experimental import pallas as pl
from jax.experimental.pallas import tpu as pltpu
from jax.sharding import PartitionSpec as P


F32 = jnp.float32
BF16 = jnp.bfloat16
N = 384
C = 128
W = 2 * N + C
MIB = 1 << 20


def unit():
    rows = lax.broadcasted_iota(jnp.int32, (C, C), 0)
    return rows == lax.broadcasted_iota(jnp.int32, (C, C), 1)


def diagonal_blocks():
    return [slice(i * C, (i + 1) * C) for i in range(3)]


def add_identity(ref):
    for at in diagonal_blocks():
        ref[at, at] = ref[at, at] + jnp.where(unit(), 1.0, 0.0)


def halves(x):
    high = x.astype(BF16)
    return high, (x - high.astype(F32)).astype(BF16)


def put_left(ref, x):
    high, low = halves(x)
    ref[:, 0:N] = high
    ref[:, N : 2 * N] = high
    ref[:, 2 * N : 3 * N] = low


def put_right(ref, x, at=0):
    high, low = halves(x)
    cols = slice(at, at + x.shape[1])
    ref[0:N, cols] = high
    ref[N : 2 * N, cols] = low
    ref[2 * N : 3 * N, cols] = high


def put_both(ref, x):
    high, low = halves(x)
    ref[:, 0:N] = high
    ref[:, N : 2 * N] = high
    ref[:, 2 * N : 3 * N] = low
    ref[:, 3 * N : 4 * N] = high


def dot(left, right):
    return jnp.dot(left, right, preferred_element_type=F32)


def dot_t(left, right):
    return lax.dot_general(
        left, right, (((1,), (1,)), ((), ())), preferred_element_type=F32
    )


def as_left(ref):
    return ref[:, 0 : 3 * N]


def as_right_t(ref):
    return ref[:, N : 4 * N]


def invert(block, out, left_e, left_p, right_e, right_p, s_e, s_2, beside=None):
    kept = sum(jnp.where(unit(), block[at, at], 0.0) for at in diagonal_blocks())
    scale = N / jnp.sum(jnp.sum(kept, axis=0, keepdims=True), axis=1, keepdims=True)
    s_e[...] = -(scale * block[...])
    add_identity(s_e)
    put_left(left_e, s_e[...])
    put_right(right_e, s_e[...])
    s_2[...] = dot(left_e[...], right_e[...])
    if beside is not None:
        beside()
    put_left(left_p, s_2[...])
    put_right(right_p, s_2[...])
    put_right(right_e, dot(left_p[...], right_p[...]))
    cube = dot(left_e[...], right_p[...])
    s_e[...] = s_e[...] + s_2[...] + cube
    add_identity(s_e)
    put_left(left_p, s_e[...])
    out[...] = scale * (s_e[...] + dot(left_p[...], right_e[...]))


INVERT_SCRATCH = [
    pltpu.VMEM((N, 3 * N), BF16),
    pltpu.VMEM((N, 3 * N), BF16),
    pltpu.VMEM((3 * N, N), BF16),
    pltpu.VMEM((3 * N, N), BF16),
    pltpu.VMEM((N, N), F32),
    pltpu.VMEM((N, N), F32),
]


def pack(out, x):
    out[0:C, :] = x[0:C, :]
    out[C : 2 * C, 0 : 2 * C] = x[C : 2 * C, C:N]
    out[C : 2 * C, 2 * C : N] = x[2 * C : N, 2 * C : N]


def unpack(out, packed):
    out[0:C, :] = packed[0:C, :]
    out[C : 2 * C, C:N] = packed[C : 2 * C, 0 : 2 * C]
    out[2 * C : N, 2 * C : N] = packed[C : 2 * C, 2 * C : N]
    out[C : 2 * C, 0:C] = packed[0:C, C : 2 * C].T
    out[2 * C : N, 0:C] = packed[0:C, 2 * C : N].T
    out[2 * C : N, C : 2 * C] = packed[C : 2 * C, C : 2 * C].T


def pack_rhs(out, x):
    for i in range(3):
        out[2 * C : N, i * C : (i + 1) * C] = x[i * C : (i + 1) * C, :]


def unpack_rhs(packed):
    return jnp.concatenate([packed[2 * C : N, i * C : (i + 1) * C] for i in range(3)], axis=0)


def first_kernel(
    diag, coup, rhs, pay, keep, u_high, inv_out, rhs_out, d_in, u_in, r_in, right, left, left_u, *rest
):
    inv_scratch, sems = rest[:6], rest[6]
    at_low = (lax.axis_index("layer") % 2) == 0
    loads = [
        pltpu.make_async_copy(diag.at[0], d_in.at[0], sems.at[0]),
        pltpu.make_async_copy(coup.at[0], u_in, sems.at[1]),
        pltpu.make_async_copy(rhs.at[0], r_in.at[0], sems.at[2]),
        pltpu.make_async_copy(diag.at[1], d_in.at[1], sems.at[3]),
        pltpu.make_async_copy(coup.at[1], u_high, sems.at[4]),
        pltpu.make_async_copy(rhs.at[1], r_in.at[1], sems.at[5]),
    ]
    for load in loads:
        load.start()
    loads[0].wait()

    def transpose_u():
        loads[1].wait()
        put_left(left_u, u_in[...].T)
        put_right(right, u_in[...], 0)

    def finish(of_x, of_d):
        invert(d_in.at[0], of_x.at[:, 0:N], *inv_scratch, beside=transpose_u)
        for load in loads[2:]:
            load.wait()
        stores = [
            pltpu.make_async_copy(of_x.at[:, 0:N], inv_out.at[0], sems.at[0]),
            pltpu.make_async_copy(r_in.at[0], rhs_out.at[0], sems.at[1]),
        ]
        for store in stores:
            store.start()
        put_left(left, of_x[:, 0:N])
        put_right(right, r_in[0], N)
        of_x[:, N:W] = dot(left[...], right[...])
        put_right(right, of_x[:, N:W])
        of_d[:, 0:N] = d_in[1] - dot(left_u[...], right[:, 0:N])
        of_d[:, 2 * N : W] = r_in[1] - dot(left_u[...], right[:, N : N + C])
        for store in stores:
            store.wait()

    @pl.when(at_low)
    def _():
        finish(keep, pay)
        pay[:, N : 2 * N] = u_high[...]

    @pl.when(jnp.logical_not(at_low))
    def _():
        finish(pay, keep)


def by_role(step, pay, recv):
    at_low = (lax.axis_index("layer") % 2) == 0

    @pl.when(at_low)
    def _():
        step(pay, recv)

    @pl.when(jnp.logical_not(at_low))
    def _():
        step(recv, pay)


def second_kernel(pay, recv, x_b, both, left, right, d_s, *inv_scratch):
    def step(of_d, of_x):
        put_both(both, of_d[:, N : 2 * N])
        put_right(right, of_x[:, 0:N])
        put_left(left, dot(as_left(both), right[...]))
        d_s[...] = of_d[:, 0:N] - dot_t(left[...], as_right_t(both))

    by_role(step, pay, recv)
    invert(d_s, x_b, *inv_scratch)


def third_kernel(keep, x_b, packed, whole, t_left, both, right):
    @pl.when((lax.axis_index("layer") % 2) == 0)
    def _():
        put_both(both, keep[:, N : 2 * N])
        put_right(right, x_b[...])
        put_left(t_left, dot(as_left(both), right[...]))
        whole[...] = keep[:, 0:N] + dot_t(t_left[...], as_right_t(both))
        pack(packed, whole)


def spread_kernel(
    t_left, pay, recv, keep, s_in, x_b, inv_in, rhs_in,
    full, packed, whole, thin, inv_out, rhs_out, both, left, right, u_b, r_b, sems
):
    del inv_in, rhs_in
    at_low = (lax.axis_index("layer") % 2) == 0
    stores = [
        pltpu.make_async_copy(x_b, inv_out.at[1], sems.at[0]),
        pltpu.make_async_copy(r_b, rhs_out.at[1], sems.at[1]),
    ]

    def step(of_d, of_x):
        put_left(left, of_d[:, N : 2 * N])
        put_right(right, of_x[:, N:W])
        u_b[...] = -dot(left[...], right[:, 0:N])
        r_b[...] = of_d[:, 2 * N : W] - dot(left[...], right[:, N : N + C])

    by_role(step, pay, recv)

    @pl.when(at_low)
    def _():
        for store in stores:
            store.start()
        put_right(right, u_b[...], 0)
        put_right(right, r_b[...], N)
        full[:, N : 2 * N] = dot(t_left[...], right[:, 0:N])
        thin[...] = keep[:, 2 * N : W] - dot(t_left[...], right[:, N : N + C])
        full[:, 0:N] = s_in[...]
        full[:, 2 * N : W] = thin[...]
        for store in stores:
            store.wait()

    @pl.when(jnp.logical_not(at_low))
    def _():
        put_both(both, u_b[...].T)
        put_right(right, x_b[...], 0)
        put_left(left, dot(as_left(both), right[:, 0:N]))
        put_right(right, r_b[...], N)
        whole[...] = keep[:, 0:N] - dot_t(left[...], as_right_t(both))
        thin[...] = keep[:, 2 * N : W] - dot(left[...], right[:, N : N + C])
        pack(packed, whole)
        pack_rhs(packed, thin)


def fourth_kernel(whole, packed_in, full, u_high, packed, x_out, t_left, both, left, right, d_s, *inv_scratch):
    @pl.when(lax.axis_index("layer") % 4 == 1)
    def _():
        put_both(both, u_high[...])
        unpack(d_s, packed_in)
        put_right(right, d_s[...])
        put_left(left, dot(as_left(both), right[...]))
        d_s[...] = whole[...] - dot_t(left[...], as_right_t(both))
        invert(d_s, x_out, *inv_scratch, beside=lambda: put_both(both, full[:, N : 2 * N]))
        put_right(right, x_out[...])
        put_left(t_left, dot(as_left(both), right[...]))
        d_s[...] = full[:, 0:N] + dot_t(t_left[...], as_right_t(both))
        pack(packed, d_s)


def rest_kernel(t_left, thin, thin_in, full, u_high, thin_out, r_out, left, right):
    @pl.when(lax.axis_index("layer") % 4 == 1)
    def _():
        put_left(left, u_high[...])
        put_right(right, thin_in[...])
        r_out[...] = thin[...] - dot(left[...], right[...])
        put_right(right, r_out[...])
        thin_out[...] = full[:, 2 * N : W] + dot(t_left[...], right[...])


def left_kernel(full, u_left, sums, both, left, right):
    @pl.when(lax.axis_index("layer") % 4 == 3)
    def _():
        put_both(both, u_left[...])
        put_right(right, full[...])
        sums[...] = dot(as_left(both), right[...])
        put_left(left, sums[:, 0:N])
        sums[:, 0:N] = dot_t(left[...], as_right_t(both))


def fifth_kernel(
    whole, thin, packed_in, sums, u_high, x_in, r_in, inv_in, rhs_in,
    whole_out, thin_out, u_both, inv_out, rhs_out,
    both, left, right, d_s, x_s, *rest
):
    del inv_in, rhs_in
    inv_scratch, sems = rest[:6], rest[6]
    place = lax.axis_index("layer") % 4

    @pl.when(place == 1)
    def _():
        stores = [
            pltpu.make_async_copy(x_in, inv_out.at[1], sems.at[0]),
            pltpu.make_async_copy(r_in, rhs_out.at[1], sems.at[1]),
        ]
        for store in stores:
            store.start()
        for store in stores:
            store.wait()

    @pl.when(place == 3)
    def _():
        unpack(d_s, packed_in)
        d_s[...] = d_s[...] - sums[:, 0:N]
        invert(d_s, x_s, *inv_scratch, beside=lambda: put_both(both, sums[:, N : 2 * N].T))
        put_right(right, x_s[...])
        put_left(left, dot(as_left(both), right[...]))
        whole_out[...] = whole[...] - dot_t(left[...], as_right_t(both))
        put_right(right, unpack_rhs(packed_in) - sums[:, 2 * N : W])
        thin_out[...] = thin[...] - dot(left[...], right[:, 0:C])
        put_both(u_both, u_high[...])


def sixth_kernel(whole, packed_in, u_both, x_out, left, right, d_s, *inv_scratch):
    @pl.when(lax.axis_index("layer") % 4 == 3)
    def _():
        unpack(d_s, packed_in)
        put_right(right, d_s[...])
        put_left(left, dot(as_left(u_both), right[...]))
        d_s[...] = whole[...] - dot_t(left[...], as_right_t(u_both))
        invert(d_s, x_out, *inv_scratch)


def last_kernel(x_in, thin, thin_in, u_both, inv_in, rhs_in, inv_out, rhs_out, right, r_s, sems):
    del inv_in, rhs_in

    @pl.when(lax.axis_index("layer") % 4 == 3)
    def _():
        inv_store = pltpu.make_async_copy(x_in, inv_out.at[1], sems.at[0])
        inv_store.start()
        put_right(right, thin_in[...])
        r_s[...] = thin[...] - dot(as_left(u_both), right[...])
        rhs_store = pltpu.make_async_copy(r_s, rhs_out.at[1], sems.at[1])
        rhs_store.start()
        inv_store.wait()
        rhs_store.wait()


def vmem():
    return pl.BlockSpec(memory_space=pltpu.VMEM)


def in_hbm():
    return pl.BlockSpec(memory_space=pltpu.HBM)


def like(*shape):
    return jax.ShapeDtypeStruct(shape, F32)


def call(kernel, outs, out_specs, in_specs, scratch, products, aliases=None):
    return pl.pallas_call(
        kernel,
        out_shape=outs,
        in_specs=in_specs,
        out_specs=out_specs,
        scratch_shapes=scratch,
        input_output_aliases=aliases or {},
        compiler_params=pltpu.CompilerParams(vmem_limit_bytes=28 * MIB),
        cost_estimate=pl.CostEstimate(
            flops=int(products * 6 * N * N * N), bytes_accessed=4 * MIB, transcendentals=0
        ),
    )


def reduce_chain(diag_block, coupling, right_side):
    size = lax.axis_size("layer")
    groups = range(size // 4)

    def send(block, route):
        return lax.ppermute(block, "layer", [(i % size, j % size) for i, j in route])

    def send_crossed(block, route):
        pairs = [(2 * (i % size) + c, 2 * (j % size) + 1 - c) for i, j in route for c in (0, 1)]
        return lax.ppermute(block, ("layer", "rhs"), pairs)

    wide = pltpu.VMEM((3 * N, W), BF16)
    mid = pltpu.VMEM((3 * N, N + C), BF16)
    tall = pltpu.VMEM((3 * N, N), BF16)
    flat = pltpu.VMEM((N, 3 * N), BF16)
    double = pltpu.VMEM((N, 4 * N), BF16)
    tile = pltpu.VMEM((N, N), F32)
    strip = pltpu.VMEM((N, C), F32)
    sems = pltpu.SemaphoreType.DMA((6,))
    outputs = (like(2, N, N), like(2, N, C))
    half_form = jax.ShapeDtypeStruct((N, 3 * N), BF16)
    triangle = like(2 * C, N)

    pay, keep, u_high, inv_out, rhs_out = call(
        first_kernel,
        (like(N, W), like(N, W), like(N, N), *outputs),
        (vmem(), vmem(), vmem(), in_hbm(), in_hbm()),
        [in_hbm()] * 3,
        [pltpu.VMEM((2, N, N), F32), tile, pltpu.VMEM((2, N, C), F32), mid, flat, flat, *INVERT_SCRATCH, sems],
        6.67,
    )(*[pltpu.with_memory_space_constraint(x, pltpu.HBM) for x in (diag_block, coupling, right_side)])
    recv = send(pay, [(i, i ^ 1) for i in range(size)])
    u_left = send(u_high, [(4 * g + 1, 4 * g + 3) for g in groups])
    x_b = call(
        second_kernel,
        like(N, N),
        vmem(),
        [vmem()] * 2,
        [double, flat, tall, tile, *INVERT_SCRATCH],
        6,
    )(pay, recv)
    packed, whole, t_left = call(
        third_kernel,
        (triangle, like(N, N), half_form),
        (vmem(),) * 3,
        [vmem()] * 2,
        [double, tall],
        2,
    )(keep, x_b)
    urgent_in = send_crossed(packed, [(4 * g + 2, 4 * g + 1) for g in groups])
    full, packed, whole, thin, inv_out, rhs_out = call(
        spread_kernel,
        (like(N, W), like(N, N), like(N, N), like(N, C), *outputs),
        (vmem(), vmem(), vmem(), vmem(), in_hbm(), in_hbm()),
        [vmem()] * 6 + [in_hbm()] * 2,
        [double, flat, mid, tile, strip, sems],
        3.33,
        {6: 4, 7: 5},
    )(t_left, pay, recv, keep, whole, x_b, inv_out, rhs_out)
    full_in = send(full, [(4 * g, 4 * g + 1) for g in groups])
    thin_in = send(thin, [(4 * g + 2, 4 * g + 1) for g in groups])
    packed_in = send(packed, [(4 * g + 1, 4 * g + 3) for g in groups])
    packed, x_3, t_left = call(
        fourth_kernel,
        (triangle, like(N, N), half_form),
        (vmem(),) * 3,
        [vmem()] * 4,
        [double, flat, tall, tile, *INVERT_SCRATCH],
        8,
    )(whole, urgent_in, full_in, u_high)
    down = [(4 * g + 5, 4 * g + 3) for g in groups]
    last_in = send_crossed(packed, down)
    down_thin, r_3 = call(
        rest_kernel,
        (like(N, C), like(N, C)),
        (vmem(),) * 2,
        [vmem()] * 5,
        [flat, pltpu.VMEM((3 * N, C), BF16)],
        0.67,
    )(t_left, thin, thin_in, full_in, u_high)
    thin_in = send(down_thin, down)
    sums = call(
        left_kernel,
        like(N, W),
        vmem(),
        [vmem()] * 2,
        [double, flat, wide],
        3.33,
    )(send(full, [(4 * g + 2, 4 * g + 3) for g in groups]), u_left)
    whole, thin, u_both, inv_out, rhs_out = call(
        fifth_kernel,
        (like(N, N), like(N, C), jax.ShapeDtypeStruct((N, 4 * N), BF16), *outputs),
        (vmem(), vmem(), vmem(), in_hbm(), in_hbm()),
        [vmem()] * 7 + [in_hbm()] * 2,
        [double, flat, tall, tile, tile, *INVERT_SCRATCH, sems],
        6.33,
        {7: 3, 8: 4},
    )(whole, thin, packed_in, sums, u_high, x_3, r_3, inv_out, rhs_out)
    x_7 = call(
        sixth_kernel,
        like(N, N),
        vmem(),
        [vmem()] * 3,
        [flat, tall, tile, *INVERT_SCRATCH],
        6,
    )(whole, last_in, u_both)
    return call(
        last_kernel,
        outputs,
        (in_hbm(), in_hbm()),
        [vmem()] * 4 + [in_hbm()] * 2,
        [pltpu.VMEM((3 * N, C), BF16), strip, sems],
        0.33,
        {4: 0, 5: 1},
    )(x_7, thin, thin_in, u_both, inv_out, rhs_out)


def solution(mesh):
    return jax.shard_map(
        reduce_chain,
        mesh=mesh,
        in_specs=(P("layer", None, None), P("layer", None, None), P("layer", None, "rhs")),
        out_specs=(P("layer", None, None), P("layer", None, "rhs")),
        check_vma=False,
    )
```

```python
import jax
import jax.numpy as jnp
from jax import lax
from jax.experimental import pallas as pl
from jax.experimental.pallas import tpu as pltpu
from jax.sharding import PartitionSpec as P


F32 = jnp.float32
BF16 = jnp.bfloat16
N = 384
C = 128
W = 2 * N + C
MIB = 1 << 20


def unit():
    rows = lax.broadcasted_iota(jnp.int32, (C, C), 0)
    return rows == lax.broadcasted_iota(jnp.int32, (C, C), 1)


def diagonal_blocks():
    return [slice(i * C, (i + 1) * C) for i in range(3)]


def add_identity(ref):
    for at in diagonal_blocks():
        ref[at, at] = ref[at, at] + jnp.where(unit(), 1.0, 0.0)


def halves(x):
    high = x.astype(BF16)
    return high, (x - high.astype(F32)).astype(BF16)


def put_left(ref, x):
    high, low = halves(x)
    ref[:, 0:N] = high
    ref[:, N : 2 * N] = high
    ref[:, 2 * N : 3 * N] = low


def put_right(ref, x, at=0):
    high, low = halves(x)
    cols = slice(at, at + x.shape[1])
    ref[0:N, cols] = high
    ref[N : 2 * N, cols] = low
    ref[2 * N : 3 * N, cols] = high


def put_both(ref, x):
    high, low = halves(x)
    ref[:, 0:N] = high
    ref[:, N : 2 * N] = high
    ref[:, 2 * N : 3 * N] = low
    ref[:, 3 * N : 4 * N] = high


def dot(left, right):
    return jnp.dot(left, right, preferred_element_type=F32)


def dot_t(left, right):
    return lax.dot_general(
        left, right, (((1,), (1,)), ((), ())), preferred_element_type=F32
    )


def as_left(ref):
    return ref[:, 0 : 3 * N]


def as_right_t(ref):
    return ref[:, N : 4 * N]


def invert(block, out, left_e, left_p, right_e, right_p, s_e, s_2, beside=None):
    kept = sum(jnp.where(unit(), block[at, at], 0.0) for at in diagonal_blocks())
    scale = N / jnp.sum(jnp.sum(kept, axis=0, keepdims=True), axis=1, keepdims=True)
    s_e[...] = -(scale * block[...])
    add_identity(s_e)
    put_left(left_e, s_e[...])
    put_right(right_e, s_e[...])
    s_2[...] = dot(left_e[...], right_e[...])
    if beside is not None:
        beside()
    put_left(left_p, s_2[...])
    put_right(right_p, s_2[...])
    put_right(right_e, dot(left_p[...], right_p[...]))
    cube = dot(left_e[...], right_p[...])
    s_e[...] = s_e[...] + s_2[...] + cube
    add_identity(s_e)
    put_left(left_p, s_e[...])
    out[...] = scale * (s_e[...] + dot(left_p[...], right_e[...]))


INVERT_SCRATCH = [
    pltpu.VMEM((N, 3 * N), BF16),
    pltpu.VMEM((N, 3 * N), BF16),
    pltpu.VMEM((3 * N, N), BF16),
    pltpu.VMEM((3 * N, N), BF16),
    pltpu.VMEM((N, N), F32),
    pltpu.VMEM((N, N), F32),
]


def pack(out, x):
    out[0:C, :] = x[0:C, :]
    out[C : 2 * C, 0 : 2 * C] = x[C : 2 * C, C:N]
    out[C : 2 * C, 2 * C : N] = x[2 * C : N, 2 * C : N]


def unpack(out, packed):
    out[0:C, :] = packed[0:C, :]
    out[C : 2 * C, C:N] = packed[C : 2 * C, 0 : 2 * C]
    out[2 * C : N, 2 * C : N] = packed[C : 2 * C, 2 * C : N]
    out[C : 2 * C, 0:C] = packed[0:C, C : 2 * C].T
    out[2 * C : N, 0:C] = packed[0:C, 2 * C : N].T
    out[2 * C : N, C : 2 * C] = packed[C : 2 * C, C : 2 * C].T


def pack_rhs(out, x):
    for i in range(3):
        out[2 * C : N, i * C : (i + 1) * C] = x[i * C : (i + 1) * C, :]


def unpack_rhs(packed):
    return jnp.concatenate([packed[2 * C : N, i * C : (i + 1) * C] for i in range(3)], axis=0)


def first_kernel(
    diag, coup, rhs, pay, keep, u_high, inv_out, rhs_out, d_in, u_in, r_in, right, left, left_u, *rest
):
    inv_scratch, sems = rest[:6], rest[6]
    at_low = (lax.axis_index("layer") % 2) == 0
    loads = [
        pltpu.make_async_copy(diag.at[0], d_in.at[0], sems.at[0]),
        pltpu.make_async_copy(coup.at[0], u_in, sems.at[1]),
        pltpu.make_async_copy(rhs.at[0], r_in.at[0], sems.at[2]),
        pltpu.make_async_copy(diag.at[1], d_in.at[1], sems.at[3]),
        pltpu.make_async_copy(coup.at[1], u_high, sems.at[4]),
        pltpu.make_async_copy(rhs.at[1], r_in.at[1], sems.at[5]),
    ]
    for load in loads:
        load.start()
    loads[0].wait()

    def transpose_u():
        loads[1].wait()
        put_left(left_u, u_in[...].T)
        put_right(right, u_in[...], 0)

    def finish(of_x, of_d):
        invert(d_in.at[0], of_x.at[:, 0:N], *inv_scratch, beside=transpose_u)
        for load in loads[2:]:
            load.wait()
        stores = [
            pltpu.make_async_copy(of_x.at[:, 0:N], inv_out.at[0], sems.at[0]),
            pltpu.make_async_copy(r_in.at[0], rhs_out.at[0], sems.at[1]),
        ]
        for store in stores:
            store.start()
        put_left(left, of_x[:, 0:N])
        put_right(right, r_in[0], N)
        of_x[:, N:W] = dot(left[...], right[...])
        put_right(right, of_x[:, N:W])
        of_d[:, 0:N] = d_in[1] - dot(left_u[...], right[:, 0:N])
        of_d[:, 2 * N : W] = r_in[1] - dot(left_u[...], right[:, N : N + C])
        for store in stores:
            store.wait()

    @pl.when(at_low)
    def _():
        finish(keep, pay)
        pay[:, N : 2 * N] = u_high[...]

    @pl.when(jnp.logical_not(at_low))
    def _():
        finish(pay, keep)


def by_role(step, pay, recv):
    at_low = (lax.axis_index("layer") % 2) == 0

    @pl.when(at_low)
    def _():
        step(pay, recv)

    @pl.when(jnp.logical_not(at_low))
    def _():
        step(recv, pay)


def second_kernel(pay, recv, x_b, both, left, right, d_s, *inv_scratch):
    def step(of_d, of_x):
        put_both(both, of_d[:, N : 2 * N])
        put_right(right, of_x[:, 0:N])
        put_left(left, dot(as_left(both), right[...]))
        d_s[...] = of_d[:, 0:N] - dot_t(left[...], as_right_t(both))

    by_role(step, pay, recv)
    invert(d_s, x_b, *inv_scratch)


def third_kernel(keep, x_b, packed, whole, t_left, both, right):
    @pl.when((lax.axis_index("layer") % 2) == 0)
    def _():
        put_both(both, keep[:, N : 2 * N])
        put_right(right, x_b[...])
        put_left(t_left, dot(as_left(both), right[...]))
        whole[...] = keep[:, 0:N] + dot_t(t_left[...], as_right_t(both))
        pack(packed, whole)


def updated(of_d, of_x, left, right, u_b, r_b):
    put_left(left, of_d[:, N : 2 * N])
    put_right(right, of_x[:, N:W])
    u_b[...] = -dot(left[...], right[:, 0:N])
    r_b[...] = of_d[:, 2 * N : W] - dot(left[...], right[:, N : N + C])


def keep_last(keep, x_b, u_b, r_b, whole, thin, both, left, right):
    put_both(both, u_b[...].T)
    put_right(right, x_b[...], 0)
    put_left(left, dot(as_left(both), right[:, 0:N]))
    put_right(right, r_b[...], N)
    whole[...] = keep[:, 0:N] - dot_t(left[...], as_right_t(both))
    thin[...] = keep[:, 2 * N : W] - dot(left[...], right[:, N : N + C])


def spread_kernel(
    t_left, pay, recv, keep, s_in, x_b, inv_in, rhs_in,
    full, packed, whole, thin, inv_out, rhs_out, both, left, right, u_b, r_b, sems
):
    del inv_in, rhs_in
    place = lax.axis_index("layer") % 4

    @pl.when(place % 2 == 0)
    def _():
        stores = [
            pltpu.make_async_copy(x_b, inv_out.at[1], sems.at[0]),
            pltpu.make_async_copy(r_b, rhs_out.at[1], sems.at[1]),
        ]
        stores[0].start()
        updated(pay, recv, left, right, u_b, r_b)
        stores[1].start()
        put_right(right, u_b[...], 0)
        put_right(right, r_b[...], N)
        full[:, N : 2 * N] = dot(t_left[...], right[:, 0:N])
        thin[...] = keep[:, 2 * N : W] - dot(t_left[...], right[:, N : N + C])
        full[:, 0:N] = s_in[...]
        full[:, 2 * N : W] = thin[...]
        for store in stores:
            store.wait()

    @pl.when(place == 1)
    def _():
        updated(recv, pay, left, right, u_b, r_b)
        keep_last(keep, x_b, u_b, r_b, whole, thin, both, left, right)
        pack(packed, whole)
        pack_rhs(packed, thin)


def fourth_kernel(whole, packed_in, full, u_high, packed, x_out, t_left, both, left, right, d_s, *inv_scratch):
    @pl.when(lax.axis_index("layer") % 4 == 1)
    def _():
        put_both(both, u_high[...])
        unpack(d_s, packed_in)
        put_right(right, d_s[...])
        put_left(left, dot(as_left(both), right[...]))
        d_s[...] = whole[...] - dot_t(left[...], as_right_t(both))
        invert(d_s, x_out, *inv_scratch, beside=lambda: put_both(both, full[:, N : 2 * N]))
        put_right(right, x_out[...])
        put_left(t_left, dot(as_left(both), right[...]))
        d_s[...] = full[:, 0:N] + dot_t(t_left[...], as_right_t(both))
        pack(packed, d_s)


def rest_kernel(t_left, thin, thin_in, full, u_high, thin_out, r_out, left, right):
    @pl.when(lax.axis_index("layer") % 4 == 1)
    def _():
        put_left(left, u_high[...])
        put_right(right, thin_in[...])
        r_out[...] = thin[...] - dot(left[...], right[...])
        put_right(right, r_out[...])
        thin_out[...] = full[:, 2 * N : W] + dot(t_left[...], right[...])


def left_kernel(full, u_left, pay, recv, keep, x_b, sums, whole, thin, both, left, right, u_b, r_b):
    @pl.when(lax.axis_index("layer") % 4 == 3)
    def _():
        updated(recv, pay, left, right, u_b, r_b)
        keep_last(keep, x_b, u_b, r_b, whole, thin, both, left, right)
        put_both(both, u_left[...])
        put_right(right, full[...])
        sums[...] = dot(as_left(both), right[...])
        put_left(left, sums[:, 0:N])
        sums[:, 0:N] = dot_t(left[...], as_right_t(both))


def fifth_kernel(
    whole, thin, packed_in, sums, u_high, x_in, r_in, inv_in, rhs_in,
    whole_out, thin_out, u_both, inv_out, rhs_out,
    both, left, right, d_s, x_s, *rest
):
    del inv_in, rhs_in
    inv_scratch, sems = rest[:6], rest[6]
    place = lax.axis_index("layer") % 4

    @pl.when(place == 1)
    def _():
        stores = [
            pltpu.make_async_copy(x_in, inv_out.at[1], sems.at[0]),
            pltpu.make_async_copy(r_in, rhs_out.at[1], sems.at[1]),
        ]
        for store in stores:
            store.start()
        for store in stores:
            store.wait()

    @pl.when(place == 3)
    def _():
        unpack(d_s, packed_in)
        d_s[...] = d_s[...] - sums[:, 0:N]
        invert(d_s, x_s, *inv_scratch, beside=lambda: put_both(both, sums[:, N : 2 * N].T))
        put_right(right, x_s[...])
        put_left(left, dot(as_left(both), right[...]))
        whole_out[...] = whole[...] - dot_t(left[...], as_right_t(both))
        put_right(right, unpack_rhs(packed_in) - sums[:, 2 * N : W])
        thin_out[...] = thin[...] - dot(left[...], right[:, 0:C])
        put_both(u_both, u_high[...])


def sixth_kernel(whole, packed_in, u_both, x_out, left, right, d_s, *inv_scratch):
    @pl.when(lax.axis_index("layer") % 4 == 3)
    def _():
        unpack(d_s, packed_in)
        put_right(right, d_s[...])
        put_left(left, dot(as_left(u_both), right[...]))
        d_s[...] = whole[...] - dot_t(left[...], as_right_t(u_both))
        invert(d_s, x_out, *inv_scratch)


def last_kernel(x_in, thin, thin_in, u_both, inv_in, rhs_in, inv_out, rhs_out, right, r_s, sems):
    del inv_in, rhs_in

    @pl.when(lax.axis_index("layer") % 4 == 3)
    def _():
        inv_store = pltpu.make_async_copy(x_in, inv_out.at[1], sems.at[0])
        inv_store.start()
        put_right(right, thin_in[...])
        r_s[...] = thin[...] - dot(as_left(u_both), right[...])
        rhs_store = pltpu.make_async_copy(r_s, rhs_out.at[1], sems.at[1])
        rhs_store.start()
        inv_store.wait()
        rhs_store.wait()


def vmem():
    return pl.BlockSpec(memory_space=pltpu.VMEM)


def in_hbm():
    return pl.BlockSpec(memory_space=pltpu.HBM)


def like(*shape):
    return jax.ShapeDtypeStruct(shape, F32)


def call(kernel, outs, out_specs, in_specs, scratch, products, aliases=None):
    return pl.pallas_call(
        kernel,
        out_shape=outs,
        in_specs=in_specs,
        out_specs=out_specs,
        scratch_shapes=scratch,
        input_output_aliases=aliases or {},
        compiler_params=pltpu.CompilerParams(vmem_limit_bytes=28 * MIB),
        cost_estimate=pl.CostEstimate(
            flops=int(products * 6 * N * N * N), bytes_accessed=4 * MIB, transcendentals=0
        ),
    )


def reduce_chain(diag_block, coupling, right_side):
    size = lax.axis_size("layer")
    groups = range(size // 4)

    def send(block, route):
        return lax.ppermute(block, "layer", [(i % size, j % size) for i, j in route])

    wide = pltpu.VMEM((3 * N, W), BF16)
    mid = pltpu.VMEM((3 * N, N + C), BF16)
    tall = pltpu.VMEM((3 * N, N), BF16)
    flat = pltpu.VMEM((N, 3 * N), BF16)
    double = pltpu.VMEM((N, 4 * N), BF16)
    tile = pltpu.VMEM((N, N), F32)
    strip = pltpu.VMEM((N, C), F32)
    sems = pltpu.SemaphoreType.DMA((6,))
    outputs = (like(2, N, N), like(2, N, C))
    half_form = jax.ShapeDtypeStruct((N, 3 * N), BF16)
    triangle = like(2 * C, N)

    pay, keep, u_high, inv_out, rhs_out = call(
        first_kernel,
        (like(N, W), like(N, W), like(N, N), *outputs),
        (vmem(), vmem(), vmem(), in_hbm(), in_hbm()),
        [in_hbm()] * 3,
        [pltpu.VMEM((2, N, N), F32), tile, pltpu.VMEM((2, N, C), F32), mid, flat, flat, *INVERT_SCRATCH, sems],
        6.67,
    )(*[pltpu.with_memory_space_constraint(x, pltpu.HBM) for x in (diag_block, coupling, right_side)])
    recv = send(pay, [(i, i ^ 1) for i in range(size)])
    u_left = send(u_high, [(4 * g + 1, 4 * g + 3) for g in groups])
    x_b = call(
        second_kernel,
        like(N, N),
        vmem(),
        [vmem()] * 2,
        [double, flat, tall, tile, *INVERT_SCRATCH],
        6,
    )(pay, recv)
    packed, whole, t_left = call(
        third_kernel,
        (triangle, like(N, N), half_form),
        (vmem(),) * 3,
        [vmem()] * 2,
        [double, tall],
        2,
    )(keep, x_b)
    urgent_in = send(packed, [(4 * g + 2, 4 * g + 1) for g in groups])
    full, packed, whole, thin, inv_out, rhs_out = call(
        spread_kernel,
        (like(N, W), like(N, N), like(N, N), like(N, C), *outputs),
        (vmem(), vmem(), vmem(), vmem(), in_hbm(), in_hbm()),
        [vmem()] * 6 + [in_hbm()] * 2,
        [double, flat, mid, tile, strip, sems],
        3.33,
        {6: 4, 7: 5},
    )(t_left, pay, recv, keep, whole, x_b, inv_out, rhs_out)
    full_in = send(full, [(4 * g, 4 * g + 1) for g in groups])
    thin_in = send(thin, [(4 * g + 2, 4 * g + 1) for g in groups])
    packed_in = send(packed, [(4 * g + 1, 4 * g + 3) for g in groups])
    packed, x_3, t_left = call(
        fourth_kernel,
        (triangle, like(N, N), half_form),
        (vmem(),) * 3,
        [vmem()] * 4,
        [double, flat, tall, tile, *INVERT_SCRATCH],
        8,
    )(whole, urgent_in, full_in, u_high)
    down = [(4 * g + 5, 4 * g + 3) for g in groups]
    crossed = [(2 * (i % size) + c, 2 * (j % size) + 1 - c) for i, j in down for c in (0, 1)]
    last_in = lax.ppermute(packed, ("layer", "rhs"), crossed)
    down_thin, r_3 = call(
        rest_kernel,
        (like(N, C), like(N, C)),
        (vmem(),) * 2,
        [vmem()] * 5,
        [flat, pltpu.VMEM((3 * N, C), BF16)],
        0.67,
    )(t_left, thin, thin_in, full_in, u_high)
    thin_in = send(down_thin, down)
    full_b = send(full, [(4 * g + 2, 4 * g + 3) for g in groups])
    sums, whole, thin = call(
        left_kernel,
        (like(N, W), like(N, N), like(N, C)),
        (vmem(),) * 3,
        [vmem()] * 6,
        [double, flat, wide, tile, strip],
        7,
    )(full_b, u_left, pay, recv, keep, x_b)
    whole, thin, u_both, inv_out, rhs_out = call(
        fifth_kernel,
        (like(N, N), like(N, C), jax.ShapeDtypeStruct((N, 4 * N), BF16), *outputs),
        (vmem(), vmem(), vmem(), in_hbm(), in_hbm()),
        [vmem()] * 7 + [in_hbm()] * 2,
        [double, flat, tall, tile, tile, *INVERT_SCRATCH, sems],
        6.33,
        {7: 3, 8: 4},
    )(whole, thin, packed_in, sums, u_high, x_3, r_3, inv_out, rhs_out)
    x_7 = call(
        sixth_kernel,
        like(N, N),
        vmem(),
        [vmem()] * 3,
        [flat, tall, tile, *INVERT_SCRATCH],
        6,
    )(whole, last_in, u_both)
    return call(
        last_kernel,
        outputs,
        (in_hbm(), in_hbm()),
        [vmem()] * 4 + [in_hbm()] * 2,
        [pltpu.VMEM((3 * N, C), BF16), strip, sems],
        0.33,
        {4: 0, 5: 1},
    )(x_7, thin, thin_in, u_both, inv_out, rhs_out)


def solution(mesh):
    return jax.shard_map(
        reduce_chain,
        mesh=mesh,
        in_specs=(P("layer", None, None), P("layer", None, None), P("layer", None, "rhs")),
        out_specs=(P("layer", None, None), P("layer", None, "rhs")),
        check_vma=False,
    )
```

```python
import jax
import jax.numpy as jnp
from jax import lax
from jax.experimental import pallas as pl
from jax.experimental.pallas import tpu as pltpu
from jax.sharding import PartitionSpec as P


F32 = jnp.float32
BF16 = jnp.bfloat16
N = 384
C = 128
W = 2 * N + C
MIB = 1 << 20


def unit():
    rows = lax.broadcasted_iota(jnp.int32, (C, C), 0)
    return rows == lax.broadcasted_iota(jnp.int32, (C, C), 1)


def diagonal_blocks():
    return [slice(i * C, (i + 1) * C) for i in range(3)]


def add_identity(ref):
    for at in diagonal_blocks():
        ref[at, at] = ref[at, at] + jnp.where(unit(), 1.0, 0.0)


def halves(x):
    high = x.astype(BF16)
    return high, (x - high.astype(F32)).astype(BF16)


def put_left(ref, x):
    high, low = halves(x)
    ref[:, 0:N] = high
    ref[:, N : 2 * N] = high
    ref[:, 2 * N : 3 * N] = low


def put_right(ref, x, at=0):
    high, low = halves(x)
    cols = slice(at, at + x.shape[1])
    ref[0:N, cols] = high
    ref[N : 2 * N, cols] = low
    ref[2 * N : 3 * N, cols] = high


def put_both(ref, x):
    high, low = halves(x)
    ref[:, 0:N] = high
    ref[:, N : 2 * N] = high
    ref[:, 2 * N : 3 * N] = low
    ref[:, 3 * N : 4 * N] = high


def dot(left, right):
    return jnp.dot(left, right, preferred_element_type=F32)


def dot_t(left, right):
    return lax.dot_general(
        left, right, (((1,), (1,)), ((), ())), preferred_element_type=F32
    )


def as_left(ref):
    return ref[:, 0 : 3 * N]


def as_right_t(ref):
    return ref[:, N : 4 * N]


def invert(block, out, left_e, left_p, right_e, right_p, s_e, s_2, beside=None):
    kept = sum(jnp.where(unit(), block[at, at], 0.0) for at in diagonal_blocks())
    scale = N / jnp.sum(jnp.sum(kept, axis=0, keepdims=True), axis=1, keepdims=True)
    s_e[...] = -(scale * block[...])
    add_identity(s_e)
    put_left(left_e, s_e[...])
    put_right(right_e, s_e[...])
    s_2[...] = dot(left_e[...], right_e[...])
    if beside is not None:
        beside()
    put_left(left_p, s_2[...])
    put_right(right_p, s_2[...])
    put_right(right_e, dot(left_p[...], right_p[...]))
    cube = dot(left_e[...], right_p[...])
    s_e[...] = s_e[...] + s_2[...] + cube
    add_identity(s_e)
    put_left(left_p, s_e[...])
    out[...] = scale * (s_e[...] + dot(left_p[...], right_e[...]))


INVERT_SCRATCH = [
    pltpu.VMEM((N, 3 * N), BF16),
    pltpu.VMEM((N, 3 * N), BF16),
    pltpu.VMEM((3 * N, N), BF16),
    pltpu.VMEM((3 * N, N), BF16),
    pltpu.VMEM((N, N), F32),
    pltpu.VMEM((N, N), F32),
]


def pack(out, x):
    out[0:C, :] = x[0:C, :]
    out[C : 2 * C, 0 : 2 * C] = x[C : 2 * C, C:N]
    out[C : 2 * C, 2 * C : N] = x[2 * C : N, 2 * C : N]


def unpack(out, packed):
    out[0:C, :] = packed[0:C, :]
    out[C : 2 * C, C:N] = packed[C : 2 * C, 0 : 2 * C]
    out[2 * C : N, 2 * C : N] = packed[C : 2 * C, 2 * C : N]
    out[C : 2 * C, 0:C] = packed[0:C, C : 2 * C].T
    out[2 * C : N, 0:C] = packed[0:C, 2 * C : N].T
    out[2 * C : N, C : 2 * C] = packed[C : 2 * C, C : 2 * C].T


def put_right_packed(ref, packed):
    blocks = {(0, j): packed[0:C, j * C : (j + 1) * C] for j in range(3)}
    blocks |= {(1, j): packed[C : 2 * C, (j - 1) * C : j * C] for j in (1, 2)}
    blocks[2, 2] = packed[C : 2 * C, 2 * C : N]
    for (i, j), x in blocks.items():
        for row, col, part in ((i, j, x), (j, i, x.T))[: 1 + (i != j)]:
            high, low = halves(part)
            at = slice(col * C, (col + 1) * C)
            for third, half in enumerate((high, low, high)):
                ref[third * N + row * C : third * N + (row + 1) * C, at] = half


def pack_rhs(out, x):
    for i in range(3):
        out[2 * C : N, i * C : (i + 1) * C] = x[i * C : (i + 1) * C, :]


def unpack_rhs(packed):
    return jnp.concatenate([packed[2 * C : N, i * C : (i + 1) * C] for i in range(3)], axis=0)


def first_kernel(
    diag, coup, rhs, pay, keep, u_high, inv_out, rhs_out, d_in, u_in, r_in, right, left, left_u, *rest
):
    inv_scratch, sems = rest[:6], rest[6]
    at_low = (lax.axis_index("layer") % 2) == 0
    loads = [
        pltpu.make_async_copy(diag.at[0], d_in.at[0], sems.at[0]),
        pltpu.make_async_copy(coup.at[0], u_in, sems.at[1]),
        pltpu.make_async_copy(rhs.at[0], r_in.at[0], sems.at[2]),
        pltpu.make_async_copy(diag.at[1], d_in.at[1], sems.at[3]),
        pltpu.make_async_copy(coup.at[1], u_high, sems.at[4]),
        pltpu.make_async_copy(rhs.at[1], r_in.at[1], sems.at[5]),
    ]
    for load in loads:
        load.start()
    loads[0].wait()

    def transpose_u():
        loads[1].wait()
        put_left(left_u, u_in[...].T)
        put_right(right, u_in[...], 0)

    def finish(of_x, of_d):
        invert(d_in.at[0], of_x.at[:, 0:N], *inv_scratch, beside=transpose_u)
        for load in loads[2:]:
            load.wait()
        stores = [
            pltpu.make_async_copy(of_x.at[:, 0:N], inv_out.at[0], sems.at[0]),
            pltpu.make_async_copy(r_in.at[0], rhs_out.at[0], sems.at[1]),
        ]
        for store in stores:
            store.start()
        put_left(left, of_x[:, 0:N])
        put_right(right, r_in[0], N)
        of_x[:, N:W] = dot(left[...], right[...])
        put_right(right, of_x[:, N:W])
        of_d[:, 0:N] = d_in[1] - dot(left_u[...], right[:, 0:N])
        of_d[:, 2 * N : W] = r_in[1] - dot(left_u[...], right[:, N : N + C])
        for store in stores:
            store.wait()

    @pl.when(at_low)
    def _():
        finish(keep, pay)
        pay[:, N : 2 * N] = u_high[...]

    @pl.when(jnp.logical_not(at_low))
    def _():
        finish(pay, keep)


def by_role(step, pay, recv):
    at_low = (lax.axis_index("layer") % 2) == 0

    @pl.when(at_low)
    def _():
        step(pay, recv)

    @pl.when(jnp.logical_not(at_low))
    def _():
        step(recv, pay)


def second_kernel(pay, recv, keep, x_b, packed, whole, t_left, both, left, right, d_s, *inv_scratch):
    def step(of_d, of_x):
        put_both(both, of_d[:, N : 2 * N])
        put_right(right, of_x[:, 0:N])
        put_left(left, dot(as_left(both), right[...]))
        d_s[...] = of_d[:, 0:N] - dot_t(left[...], as_right_t(both))

    by_role(step, pay, recv)
    invert(d_s, x_b, *inv_scratch)

    @pl.when((lax.axis_index("layer") % 2) == 0)
    def _():
        put_both(both, keep[:, N : 2 * N])
        put_right(right, x_b[...])
        put_left(t_left, dot(as_left(both), right[...]))
        whole[...] = keep[:, 0:N] + dot_t(t_left[...], as_right_t(both))
        pack(packed, whole)


def updated(of_d, of_x, left, right, u_b, r_b):
    put_left(left, of_d[:, N : 2 * N])
    put_right(right, of_x[:, N:W])
    u_b[...] = -dot(left[...], right[:, 0:N])
    r_b[...] = of_d[:, 2 * N : W] - dot(left[...], right[:, N : N + C])


def keep_last(keep, x_b, u_b, r_b, whole, thin, both, left, right):
    put_both(both, u_b[...].T)
    put_right(right, x_b[...], 0)
    put_left(left, dot(as_left(both), right[:, 0:N]))
    put_right(right, r_b[...], N)
    whole[...] = keep[:, 0:N] - dot_t(left[...], as_right_t(both))
    thin[...] = keep[:, 2 * N : W] - dot(left[...], right[:, N : N + C])


def spread_kernel(
    t_left, pay, recv, keep, s_in, x_b, inv_in, rhs_in,
    full, packed, whole, thin, inv_out, rhs_out, both, left, right, u_b, r_b, sems
):
    del inv_in, rhs_in
    place = lax.axis_index("layer") % 4

    @pl.when(place % 2 == 0)
    def _():
        stores = [
            pltpu.make_async_copy(x_b, inv_out.at[1], sems.at[0]),
            pltpu.make_async_copy(r_b, rhs_out.at[1], sems.at[1]),
        ]
        stores[0].start()
        updated(pay, recv, left, right, u_b, r_b)
        stores[1].start()
        put_right(right, u_b[...], 0)
        put_right(right, r_b[...], N)
        full[:, N : 2 * N] = dot(t_left[...], right[:, 0:N])
        thin[...] = keep[:, 2 * N : W] - dot(t_left[...], right[:, N : N + C])
        full[:, 0:N] = s_in[...]
        full[:, 2 * N : W] = thin[...]
        for store in stores:
            store.wait()

    @pl.when(place == 1)
    def _():
        updated(recv, pay, left, right, u_b, r_b)
        keep_last(keep, x_b, u_b, r_b, whole, thin, both, left, right)
        pack(packed, whole)
        pack_rhs(packed, thin)


def fourth_kernel(whole, packed_in, full, u_high, packed, x_out, t_left, both, left, right, d_s, *inv_scratch):
    @pl.when(lax.axis_index("layer") % 4 == 1)
    def _():
        put_both(both, u_high[...])
        put_right_packed(right, packed_in)
        put_left(left, dot(as_left(both), right[...]))
        d_s[...] = whole[...] - dot_t(left[...], as_right_t(both))
        invert(d_s, x_out, *inv_scratch, beside=lambda: put_both(both, full[:, N : 2 * N]))
        put_right(right, x_out[...])
        put_left(t_left, dot(as_left(both), right[...]))
        d_s[...] = full[:, 0:N] + dot_t(t_left[...], as_right_t(both))
        pack(packed, d_s)


def rest_kernel(t_left, thin, thin_in, full, u_high, thin_out, r_out, left, right):
    @pl.when(lax.axis_index("layer") % 4 == 1)
    def _():
        put_left(left, u_high[...])
        put_right(right, thin_in[...])
        r_out[...] = thin[...] - dot(left[...], right[...])
        put_right(right, r_out[...])
        thin_out[...] = full[:, 2 * N : W] + dot(t_left[...], right[...])


def left_kernel(full, u_left, pay, recv, keep, x_b, sums, whole, thin, both, left, right, u_b, r_b):
    @pl.when(lax.axis_index("layer") % 4 == 3)
    def _():
        updated(recv, pay, left, right, u_b, r_b)
        keep_last(keep, x_b, u_b, r_b, whole, thin, both, left, right)
        put_both(both, u_left[...])
        put_right(right, full[...])
        sums[...] = dot(as_left(both), right[...])
        put_left(left, sums[:, 0:N])
        sums[:, 0:N] = dot_t(left[...], as_right_t(both))


def fifth_kernel(
    whole, thin, packed_in, sums, u_high, x_in, r_in, inv_in, rhs_in,
    whole_out, thin_out, u_both, inv_out, rhs_out,
    both, left, right, d_s, x_s, *rest
):
    del inv_in, rhs_in
    inv_scratch, sems = rest[:6], rest[6]
    place = lax.axis_index("layer") % 4

    @pl.when(place == 1)
    def _():
        stores = [
            pltpu.make_async_copy(x_in, inv_out.at[1], sems.at[0]),
            pltpu.make_async_copy(r_in, rhs_out.at[1], sems.at[1]),
        ]
        for store in stores:
            store.start()
        for store in stores:
            store.wait()

    @pl.when(place == 3)
    def _():
        unpack(d_s, packed_in)
        d_s[...] = d_s[...] - sums[:, 0:N]
        invert(d_s, x_s, *inv_scratch, beside=lambda: put_both(both, sums[:, N : 2 * N].T))
        put_right(right, x_s[...])
        put_left(left, dot(as_left(both), right[...]))
        whole_out[...] = whole[...] - dot_t(left[...], as_right_t(both))
        put_right(right, unpack_rhs(packed_in) - sums[:, 2 * N : W])
        thin_out[...] = thin[...] - dot(left[...], right[:, 0:C])
        put_both(u_both, u_high[...])


def sixth_kernel(whole, packed_in, u_both, x_out, left, right, d_s, *inv_scratch):
    @pl.when(lax.axis_index("layer") % 4 == 3)
    def _():
        put_right_packed(right, packed_in)
        put_left(left, dot(as_left(u_both), right[...]))
        d_s[...] = whole[...] - dot_t(left[...], as_right_t(u_both))
        invert(d_s, x_out, *inv_scratch)


def last_kernel(x_in, thin, thin_in, u_both, inv_in, rhs_in, inv_out, rhs_out, right, r_s, sems):
    del inv_in, rhs_in

    @pl.when(lax.axis_index("layer") % 4 == 3)
    def _():
        inv_store = pltpu.make_async_copy(x_in, inv_out.at[1], sems.at[0])
        inv_store.start()
        put_right(right, thin_in[...])
        r_s[...] = thin[...] - dot(as_left(u_both), right[...])
        rhs_store = pltpu.make_async_copy(r_s, rhs_out.at[1], sems.at[1])
        rhs_store.start()
        inv_store.wait()
        rhs_store.wait()


def vmem():
    return pl.BlockSpec(memory_space=pltpu.VMEM)


def in_hbm():
    return pl.BlockSpec(memory_space=pltpu.HBM)


def like(*shape):
    return jax.ShapeDtypeStruct(shape, F32)


def call(kernel, outs, out_specs, in_specs, scratch, products, aliases=None):
    return pl.pallas_call(
        kernel,
        out_shape=outs,
        in_specs=in_specs,
        out_specs=out_specs,
        scratch_shapes=scratch,
        input_output_aliases=aliases or {},
        compiler_params=pltpu.CompilerParams(vmem_limit_bytes=28 * MIB),
        cost_estimate=pl.CostEstimate(
            flops=int(products * 6 * N * N * N), bytes_accessed=4 * MIB, transcendentals=0
        ),
    )


def reduce_chain(diag_block, coupling, right_side):
    size = lax.axis_size("layer")
    groups = range(size // 4)

    def send(block, route):
        return lax.ppermute(block, "layer", [(i % size, j % size) for i, j in route])

    wide = pltpu.VMEM((3 * N, W), BF16)
    mid = pltpu.VMEM((3 * N, N + C), BF16)
    tall = pltpu.VMEM((3 * N, N), BF16)
    flat = pltpu.VMEM((N, 3 * N), BF16)
    double = pltpu.VMEM((N, 4 * N), BF16)
    tile = pltpu.VMEM((N, N), F32)
    strip = pltpu.VMEM((N, C), F32)
    sems = pltpu.SemaphoreType.DMA((6,))
    outputs = (like(2, N, N), like(2, N, C))
    half_form = jax.ShapeDtypeStruct((N, 3 * N), BF16)
    triangle = like(2 * C, N)

    pay, keep, u_high, inv_out, rhs_out = call(
        first_kernel,
        (like(N, W), like(N, W), like(N, N), *outputs),
        (vmem(), vmem(), vmem(), in_hbm(), in_hbm()),
        [in_hbm()] * 3,
        [pltpu.VMEM((2, N, N), F32), tile, pltpu.VMEM((2, N, C), F32), mid, flat, flat, *INVERT_SCRATCH, sems],
        6.67,
    )(*[pltpu.with_memory_space_constraint(x, pltpu.HBM) for x in (diag_block, coupling, right_side)])
    recv = send(pay, [(i, i ^ 1) for i in range(size)])
    u_left = send(u_high, [(4 * g + 1, 4 * g + 3) for g in groups])
    x_b, packed, whole, t_left = call(
        second_kernel,
        (like(N, N), triangle, like(N, N), half_form),
        (vmem(),) * 4,
        [vmem()] * 3,
        [double, flat, tall, tile, *INVERT_SCRATCH],
        8,
    )(pay, recv, keep)
    urgent_in = send(packed, [(4 * g + 2, 4 * g + 1) for g in groups])
    full, packed, whole, thin, inv_out, rhs_out = call(
        spread_kernel,
        (like(N, W), like(N, N), like(N, N), like(N, C), *outputs),
        (vmem(), vmem(), vmem(), vmem(), in_hbm(), in_hbm()),
        [vmem()] * 6 + [in_hbm()] * 2,
        [double, flat, mid, tile, strip, sems],
        3.33,
        {6: 4, 7: 5},
    )(t_left, pay, recv, keep, whole, x_b, inv_out, rhs_out)
    full_in = send(full, [(4 * g, 4 * g + 1) for g in groups])
    thin_in = send(thin, [(4 * g + 2, 4 * g + 1) for g in groups])
    packed_in = send(packed, [(4 * g + 1, 4 * g + 3) for g in groups])
    packed, x_3, t_left = call(
        fourth_kernel,
        (triangle, like(N, N), half_form),
        (vmem(),) * 3,
        [vmem()] * 4,
        [double, flat, tall, tile, *INVERT_SCRATCH],
        8,
    )(whole, urgent_in, full_in, u_high)
    down = [(4 * g + 5, 4 * g + 3) for g in groups]
    crossed = [(2 * (i % size) + c, 2 * (j % size) + 1 - c) for i, j in down for c in (0, 1)]
    last_in = lax.ppermute(packed, ("layer", "rhs"), crossed)
    down_thin, r_3 = call(
        rest_kernel,
        (like(N, C), like(N, C)),
        (vmem(),) * 2,
        [vmem()] * 5,
        [flat, pltpu.VMEM((3 * N, C), BF16)],
        0.67,
    )(t_left, thin, thin_in, full_in, u_high)
    thin_in = send(down_thin, down)
    full_b = send(full, [(4 * g + 2, 4 * g + 3) for g in groups])
    sums, whole, thin = call(
        left_kernel,
        (like(N, W), like(N, N), like(N, C)),
        (vmem(),) * 3,
        [vmem()] * 6,
        [double, flat, wide, tile, strip],
        7,
    )(full_b, u_left, pay, recv, keep, x_b)
    whole, thin, u_both, inv_out, rhs_out = call(
        fifth_kernel,
        (like(N, N), like(N, C), jax.ShapeDtypeStruct((N, 4 * N), BF16), *outputs),
        (vmem(), vmem(), vmem(), in_hbm(), in_hbm()),
        [vmem()] * 7 + [in_hbm()] * 2,
        [double, flat, tall, tile, tile, *INVERT_SCRATCH, sems],
        6.33,
        {7: 3, 8: 4},
    )(whole, thin, packed_in, sums, u_high, x_3, r_3, inv_out, rhs_out)
    x_7 = call(
        sixth_kernel,
        like(N, N),
        vmem(),
        [vmem()] * 3,
        [flat, tall, tile, *INVERT_SCRATCH],
        6,
    )(whole, last_in, u_both)
    return call(
        last_kernel,
        outputs,
        (in_hbm(), in_hbm()),
        [vmem()] * 4 + [in_hbm()] * 2,
        [pltpu.VMEM((3 * N, C), BF16), strip, sems],
        0.33,
        {4: 0, 5: 1},
    )(x_7, thin, thin_in, u_both, inv_out, rhs_out)


def solution(mesh):
    return jax.shard_map(
        reduce_chain,
        mesh=mesh,
        in_specs=(P("layer", None, None), P("layer", None, None), P("layer", None, "rhs")),
        out_specs=(P("layer", None, None), P("layer", None, "rhs")),
        check_vma=False,
    )
```
